128 devices in a mesh: samp: 8 (over x, y_hi), probe: 16 (over y_lo, z, core).
Axes of the slice: x: 4, y: 4 (y_hi: 2, y_lo: 2; y = y_hi * 2 + y_lo), z: 4, core: 2. Of those that a mesh axis runs over, the one named last changes fastest.
Arguments:
- methyl: bfloat16 [8192, 32768], P('samp', 'probe'), may hold values from -0.25 to 1.25
- atlas: bfloat16 [64, 32768], P(None, 'probe'), may hold values from 0 to 1, as said below
- panel_ids: int32 [64], replicated, may hold values from 0 to 63, each once
Outputs:
- relmat: float32 [3, 8192, 1024], P(None, 'samp', 'probe')
- scores: float32 [32, 8192], P(None, ('samp', 'probe'))
The draws below stay inside these ranges and needn't reach their ends.
Inputs may be any that keep to these rules, and one draw needn't show every extreme that they name: atlas values are beta values between 0 and 1.
All inputs are finite; a program needn't handle non-finite values.
Results may differ from the reference program's by a relative error of at most 0.003.
Values may be sent and summed in bfloat16 or wider, within the bound.
A program may use at most 128 MiB of HBM per device.

```python
import jax
import jax.numpy as jnp
from jax import lax

K = 32
ATLAS = 64
PANEL = 1024
ITERS = 128
PANELS = 8
SAMPLES = 8192
PROBES = 32768


def atlas_values(key):
    state_key, level_key = jax.random.split(jax.random.fold_in(key, 7101))
    methylated = jax.random.uniform(state_key, (ATLAS, PROBES), jnp.float32) < 0.25
    levels = jax.random.uniform(level_key, (2, ATLAS, PROBES), jnp.float32)
    high_level = 0.74 + 0.24 * levels[0]
    low_level = 0.02 + 0.14 * levels[1]
    return jnp.where(methylated, high_level, low_level)


def draw_atlas(key, part):
    return atlas_values(key).astype(jnp.bfloat16)


def draw_methyl(key, part):
    profiles = atlas_values(key).astype(jnp.bfloat16).astype(jnp.float32)
    mix_key, noise_key, absent_key = jax.random.split(jax.random.fold_in(key, 7202), 3)
    present = jax.random.uniform(absent_key, (SAMPLES, ATLAS), jnp.float32) < 0.55
    position = jnp.arange(PROBES, dtype=jnp.float32) / PROBES
    logits = jax.random.normal(mix_key, (SAMPLES, ATLAS), jnp.float32)
    noise = 0.08 * jax.random.normal(noise_key, (SAMPLES, PROBES), jnp.float32)
    gain = 0.125 * jnp.power(8.0, position)
    shares = jax.nn.softmax(jnp.where(present, logits, -1000000000.0), axis=1)
    values = (jnp.dot(shares, profiles, precision=lax.Precision.HIGHEST) + noise) * gain[None, :]
    return jnp.clip(values, -0.25, 1.25).astype(jnp.bfloat16)


def setup_inputs(seed: int = 0) -> dict:
    splits = jax.random.split(jax.random.key(seed), 4)
    methyl = draw_methyl(jax.random.fold_in(splits[3], 71), 0)
    atlas = draw_atlas(jax.random.fold_in(splits[3], 71), 0)
    panel_ids = jax.random.permutation(splits[2], ATLAS).astype(jnp.int32)
    return {"methyl": methyl, "atlas": atlas, "panel_ids": panel_ids}


def ridge_solve(wgram, cross, ridge):
    eye = jnp.eye(wgram.shape[0], dtype=wgram.dtype)
    factor = jnp.linalg.cholesky(wgram + ridge * eye)
    middle = lax.linalg.triangular_solve(factor, cross, left_side=True, lower=True)
    return lax.linalg.triangular_solve(factor, middle, left_side=True, lower=True, transpose_a=True)

def reference(methyl, atlas, panel_ids):
    selector = (panel_ids[:K, None] == jnp.arange(ATLAS, dtype=jnp.int32)[None, :]).astype(jnp.bfloat16)
    panel = jnp.dot(selector.astype(jnp.float32), atlas.astype(jnp.float32), preferred_element_type=jnp.float32).astype(jnp.bfloat16)
    gram = jnp.dot(panel.astype(jnp.float32), panel.T.astype(jnp.float32), preferred_element_type=jnp.float32)
    proj = lax.dot_general(panel.astype(jnp.float32), methyl.astype(jnp.float32), (((1,), (1,)), ((), ())), preferred_element_type=jnp.float32)
    step_rate = 1.0 / jnp.trace(gram)

    def descend(turn_index, weights):
        grad_term = jnp.dot(gram, weights, precision=lax.Precision.HIGHEST) - proj
        return jnp.maximum(weights - step_rate * grad_term, 0.0)
    weights = lax.fori_loop(0, ITERS, descend, jnp.full(proj.shape, 1.0 / K, jnp.float32))
    scores = K * weights
    design = weights.astype(jnp.bfloat16)
    cross = jnp.dot(design.astype(jnp.float32), methyl.astype(jnp.float32), preferred_element_type=jnp.float32)
    wgram = jnp.dot(design.astype(jnp.float32), design.T.astype(jnp.float32), preferred_element_type=jnp.float32)
    loadings = ridge_solve(wgram, cross, 0.0001 * SAMPLES)
    fitted = lax.dot_general(design.astype(jnp.float32), loadings, (((0,), (0,)), ((), ())), precision=lax.Precision.HIGHEST)
    residual = methyl.astype(jnp.float32) - fitted
    spread = lax.optimization_barrier(jnp.sum(residual * residual, axis=0))
    zscore = (residual * lax.rsqrt(spread / SAMPLES + 1e-06)).astype(jnp.bfloat16)
    blocks = zscore.reshape(PANELS, PANEL, PROBES)

    def tiles_of(index):
        first_block = blocks[index]
        before = blocks[(index + PANELS - 1) % PANELS]
        after = blocks[(index + 1) % PANELS]
        return jnp.stack([lax.dot_general(first_block.astype(jnp.float32), first_block.astype(jnp.float32), (((1,), (1,)), ((), ())), preferred_element_type=jnp.float32), lax.dot_general(first_block.astype(jnp.float32), before.astype(jnp.float32), (((1,), (1,)), ((), ())), preferred_element_type=jnp.float32), lax.dot_general(first_block.astype(jnp.float32), after.astype(jnp.float32), (((1,), (1,)), ((), ())), preferred_element_type=jnp.float32)])
    tiles = lax.map(tiles_of, jnp.arange(PANELS, dtype=jnp.int32))
    tiles = jnp.transpose(tiles, (1, 0, 2, 3)).reshape(3, SAMPLES, PANEL)
    return (tiles / PROBES, scores)
```

```python
import functools

import jax
import jax.numpy as jnp
from jax import lax
from jax.experimental import pallas as pl
from jax.experimental.pallas import tpu as pltpu
from jax.sharding import PartitionSpec as P

K = 32
ITERS = 128
MESH = pl.DeviceIdType.MESH
F32 = jnp.float32
BF16 = jnp.bfloat16


def dot(a, b, dims=((1,), (0,))):
    return lax.dot_general(a, b, (dims, ((), ())), preferred_element_type=F32)


def copy_to(src, dst, send_sem, recv_sem, axis, peer):
    return pltpu.make_async_remote_copy(
        src_ref=src, dst_ref=dst, send_sem=send_sem, recv_sem=recv_sem,
        device_id={axis: peer}, device_id_type=MESH,
    )


def exchange_start(src_of, dst, send_sem, recv_sem, axis, peers, me):
    def body(step, carry):
        peer = lax.rem(me + step, peers)
        copy_to(src_of(peer), dst.at[me], send_sem.at[peer], recv_sem.at[me], axis, peer).start()
        return carry
    lax.fori_loop(1, peers, body, 0)


def exchange_wait(src_of, dst, send_sem, recv_sem, axis, peers, me):
    def body(step, carry):
        peer = lax.rem(me + step, peers)
        copy = copy_to(src_of(peer), dst.at[peer], send_sem.at[peer], recv_sem.at[peer], axis, peer)
        copy.wait_recv()
        copy.wait_send()
        return carry
    lax.fori_loop(1, peers, body, 0)


def split3(value):
    high = value.astype(BF16)
    rest = value - high.astype(F32)
    mid = rest.astype(BF16)
    low = (rest - mid.astype(F32)).astype(BF16)
    return high, mid, low


def chain_kernel(
    samps, probes_n, samples,
    methyl, atlas, ids, scores, zout, dout,
    pmsg, prcv, gcol, dmsg, drcv, cmsg, crcv, lmsg, lrcv, resid, smsg, srcv, lsplit,
    psem, prsem, dsem, drsem, csem, crsem, lsem, lrsem, ssem, srsem,
):
    me_p = lax.axis_index("probe")
    me_s = lax.axis_index("samp")
    rows, cols = methyl.shape
    share = rows // probes_n
    width = cols // samps

    barrier = pltpu.get_barrier_semaphore()

    def greet(axis, peers, me):
        def body(step, carry):
            pl.semaphore_signal(
                barrier, inc=1, device_id={axis: lax.rem(me + step, peers)}, device_id_type=MESH
            )
            return carry
        lax.fori_loop(1, peers, body, 0)
    greet("probe", probes_n, me_p)
    greet("samp", samps, me_s)

    kinds = atlas.shape[0]
    select_t = (lax.broadcasted_iota(jnp.int32, (kinds, kinds), 0) == ids[...]).astype(F32)
    selector = select_t.T[:K].astype(BF16)
    panel = dot(selector, atlas[...]).astype(BF16)
    gram_part = dot(panel, panel, ((1,), (1,)))
    pad = jnp.zeros((K, 128 - share - K), F32)

    def project(step, carry):
        block = methyl[pl.ds(pl.multiple_of(step * 2 * share, 2 * share), 2 * share), :]
        part = dot(panel, block, ((1,), (1,)))
        pmsg[2 * step] = jnp.concatenate([part[:, :share], gram_part, pad], axis=1)
        pmsg[2 * step + 1] = jnp.concatenate([part[:, share:], gram_part, pad], axis=1)
        return carry
    lax.fori_loop(0, probes_n // 2, project, 0)

    pl.semaphore_wait(barrier, probes_n - 1 + samps - 1)
    from_p = lambda peer: pmsg.at[peer]
    exchange_start(from_p, prcv, psem, prsem, "probe", probes_n, me_p)
    prcv[me_p] = pmsg[me_p]
    exchange_wait(from_p, prcv, psem, prsem, "probe", probes_n, me_p)
    total = prcv[0]
    for peer in range(1, probes_n):
        total = total + prcv[peer]
    gram = total[:, share:share + K]
    proj = total[:, :share]

    diag = lax.broadcasted_iota(jnp.int32, (K, K), 0) == lax.broadcasted_iota(jnp.int32, (K, K), 1)
    trace = jnp.sum(jnp.where(diag, gram, 0.0), axis=(0, 1), keepdims=True)
    rate = 1.0 / trace
    scaled = gram * rate
    half = K // 2
    left_k = lax.broadcasted_iota(jnp.int32, (K, 128), 1) < share
    for k in range(half):
        gcol[k] = jnp.where(
            left_k,
            jnp.broadcast_to(scaled[:, k:k + 1], (K, 128)),
            jnp.broadcast_to(scaled[:, half + k:half + k + 1], (K, 128)),
        )
    goal = jnp.concatenate([proj[:half], proj[half:]], axis=1) * rate
    left = lax.broadcasted_iota(jnp.int32, (half, 128), 1) < share

    def descend(step, state):
        sums = [None, None]
        for k in range(half):
            term = gcol[k] * jnp.broadcast_to(state[k:k + 1, :], (K, 128))
            sums[k % 2] = term if sums[k % 2] is None else sums[k % 2] + term
        acc = sums[0] + sums[1]
        keep = jnp.where(left, acc[:half], acc[half:])
        other = jnp.where(left, acc[half:], acc[:half])
        grad = keep + pltpu.roll(other, share, axis=1) - goal
        return jnp.maximum(state - grad, 0.0)
    state = lax.fori_loop(0, ITERS, descend, jnp.full((half, 128), 1.0 / K, F32))
    weights = jnp.concatenate([state[:, :share], state[:, share:]], axis=0)
    scores[...] = weights * float(K)

    four = jnp.concatenate([weights] * 4, axis=0)
    wide = jnp.concatenate([four, jnp.zeros((4 * K, 128 - share), F32)], axis=1)
    dmsg[...] = wide.T[:share].astype(BF16)
    from_d = lambda peer: dmsg
    exchange_start(from_d, drcv, dsem, drsem, "probe", probes_n, me_p)
    drcv[me_p] = dmsg[...]
    exchange_wait(from_d, drcv, dsem, drsem, "probe", probes_n, me_p)
    design4 = drcv[...].reshape(rows, 4 * K)
    dout[...] = design4
    design = design4.astype(F32).T[:K].astype(BF16)

    wgram_part = dot(design, design, ((1,), (1,)))
    wpad = jnp.concatenate([wgram_part, jnp.zeros((K, 128 - K), F32)], axis=1)

    def crossing(step, carry):
        block = methyl[:, pl.ds(pl.multiple_of(step * width, width), width)]
        cmsg[step] = jnp.concatenate([dot(design, block), wpad], axis=1)
        return carry
    lax.fori_loop(0, samps, crossing, 0)
    from_c = lambda peer: cmsg.at[peer]
    exchange_start(from_c, crcv, csem, crsem, "samp", samps, me_s)
    crcv[me_s] = cmsg[me_s]
    exchange_wait(from_c, crcv, csem, crsem, "samp", samps, me_s)
    both = crcv[0]
    for peer in range(1, samps):
        both = both + crcv[peer]

    matrix = both[:, width:]
    row_id = lax.broadcasted_iota(jnp.int32, (K, 128), 0)
    lane_id = lax.broadcasted_iota(jnp.int32, (K, 128), 1)
    matrix = matrix + jnp.where(row_id == lane_id, 0.0001 * samples, 0.0)
    right = both[:, :width]
    row_w = lax.broadcasted_iota(jnp.int32, (K, 1), 0)
    for k in range(K):
        column = matrix[:, k:k + 1]
        pivot = 1.0 / matrix[k:k + 1, k:k + 1]
        factor = jnp.where(row_w == k, 0.0, column * pivot)
        matrix_row = matrix[k:k + 1, :]
        right_row = right[k:k + 1, :]
        matrix = matrix - factor * matrix_row
        right = right - factor * right_row
    pivots = jnp.sum(jnp.where(row_id == lane_id, matrix, 0.0), axis=1, keepdims=True)
    lmsg[...] = right / pivots
    from_l = lambda peer: lmsg
    exchange_start(from_l, lrcv, lsem, lrsem, "samp", samps, me_s)
    lrcv[me_s] = lmsg[...]
    exchange_wait(from_l, lrcv, lsem, lrsem, "samp", samps, me_s)

    def residue(step, carry):
        high, mid, low = split3(lrcv[step])
        stacked = jnp.concatenate([high, mid, low, jnp.zeros_like(low)], axis=0)
        at = pl.ds(pl.multiple_of(step * width, width), width)
        lsplit[:, at] = stacked
        sums = jnp.zeros((1, width), F32)
        for r in range(0, rows, 256):
            res = methyl[r:r + 256, at].astype(F32) - dot(drcv_rows(drcv, r, 256), stacked)
            resid[r:r + 256, at] = res
            sums = sums + jnp.sum(res * res, axis=0, keepdims=True)
        smsg[:, at] = sums
        return carry

    def drcv_rows(ref, start, count):
        return ref[start // share:(start + count) // share].reshape(count, 4 * K)
    lax.fori_loop(0, samps, residue, 0)
    from_s = lambda peer: smsg
    exchange_start(from_s, srcv, ssem, srsem, "samp", samps, me_s)
    srcv[me_s] = smsg[...]
    exchange_wait(from_s, srcv, ssem, srsem, "samp", samps, me_s)
    spread = srcv[0]
    for peer in range(1, samps):
        spread = spread + srcv[peer]
    smsg[...] = lax.rsqrt(spread * (1.0 / samples) + 1e-06)

    def normalize(step, carry):
        at = pl.ds(pl.multiple_of(step * width, width), width)
        zout[:, at] = (resid[:, at] * smsg[:, at]).astype(BF16)
        return carry
    lax.fori_loop(0, samps, normalize, 0)


def chain(mesh, methyl, atlas, panel_ids):
    samps, probes_n = mesh.shape["samp"], mesh.shape["probe"]
    rows, cols = methyl.shape
    share, width = rows // probes_n, cols // samps
    vmem = pl.BlockSpec(memory_space=pltpu.VMEM)
    dma = pltpu.SemaphoreType.DMA
    return pl.pallas_call(
        functools.partial(chain_kernel, samps, probes_n, rows * samps),
        out_shape=(
            jax.ShapeDtypeStruct((K, share), F32),
            jax.ShapeDtypeStruct((rows, cols), BF16),
            jax.ShapeDtypeStruct((rows, 4 * K), BF16),
        ),
        in_specs=[vmem] * 3,
        out_specs=(vmem,) * 3,
        scratch_shapes=[
            pltpu.VMEM((probes_n, K, 128), F32),
            pltpu.VMEM((probes_n, K, 128), F32),
            pltpu.VMEM((K // 2, K, 128), F32),
            pltpu.VMEM((share, 4 * K), BF16),
            pltpu.VMEM((probes_n, share, 4 * K), BF16),
            pltpu.VMEM((samps, K, width + 128), F32),
            pltpu.VMEM((samps, K, width + 128), F32),
            pltpu.VMEM((K, width), F32),
            pltpu.VMEM((samps, K, width), F32),
            pltpu.VMEM((rows, cols), F32),
            pltpu.VMEM((1, cols), F32),
            pltpu.VMEM((samps, 1, cols), F32),
            pltpu.VMEM((4 * K, cols), BF16),
            dma((probes_n,)), dma((probes_n,)), dma((probes_n,)), dma((probes_n,)),
            dma((samps,)), dma((samps,)), dma((samps,)), dma((samps,)), dma((samps,)), dma((samps,)),
        ],
        compiler_params=pltpu.CompilerParams(
            collective_id=0, has_side_effects=True, vmem_limit_bytes=48 * 1024 * 1024
        ),
        name="chain",
    )(methyl, atlas, panel_ids.reshape(1, -1))


def shifted(value, axis, by):
    peers = lax.axis_size(axis)
    return lax.ppermute(value, axis, [(i, (i + by) % peers) for i in range(peers)])


def tile_product(first_block, other_block):
    return dot(first_block, other_block, ((1,), (1,)))


def solution(mesh):
    def body(methyl, atlas, panel_ids):
        probes = methyl.shape[1] * mesh.shape["probe"]
        scores, zscore, design = chain(mesh, methyl, atlas, panel_ids)
        before = shifted(zscore, "samp", 1)
        after = shifted(zscore, "samp", -1)
        tile_terms = jnp.stack(
            [tile_product(zscore, zscore), tile_product(zscore, before), tile_product(zscore, after)]
        )
        tile_totals = lax.psum_scatter(tile_terms, "probe", scatter_dimension=2, tiled=True)
        return (tile_totals / probes, scores)

    return jax.shard_map(
        body,
        mesh=mesh,
        in_specs=(P("samp", "probe"), P(None, "probe"), P()),
        out_specs=(P(None, "samp", "probe"), P(None, ("samp", "probe"))),
        check_vma=False,
    )
```

```python
import functools

import jax
import jax.numpy as jnp
from jax import lax
from jax.experimental import pallas as pl
from jax.experimental.pallas import tpu as pltpu
from jax.sharding import PartitionSpec as P

K = 32
ITERS = 128
GROUP = 16
MESH = pl.DeviceIdType.MESH
F32 = jnp.float32
BF16 = jnp.bfloat16


def dot(a, b, dims=((1,), (0,))):
    return lax.dot_general(a, b, (dims, ((), ())), preferred_element_type=F32)


def copy_to(src, dst, send_sem, recv_sem, axis, peer):
    return pltpu.make_async_remote_copy(
        src_ref=src, dst_ref=dst, send_sem=send_sem, recv_sem=recv_sem,
        device_id={axis: peer}, device_id_type=MESH,
    )


def exchange_start(src_of, dst, send_sem, recv_sem, axis, peers, me):
    def body(step, carry):
        peer = lax.rem(me + step, peers)
        copy_to(src_of(peer), dst.at[me], send_sem.at[peer], recv_sem.at[me], axis, peer).start()
        return carry
    lax.fori_loop(1, peers, body, 0)


def exchange_wait(src_of, dst, send_sem, recv_sem, axis, peers, me):
    def body(step, carry):
        peer = lax.rem(me + step, peers)
        copy = copy_to(src_of(peer), dst.at[peer], send_sem.at[peer], recv_sem.at[peer], axis, peer)
        copy.wait_recv()
        copy.wait_send()
        return carry
    lax.fori_loop(1, peers, body, 0)


def split3(value):
    high = value.astype(BF16)
    rest = value - high.astype(F32)
    mid = rest.astype(BF16)
    low = (rest - mid.astype(F32)).astype(BF16)
    return high, mid, low


def program_kernel(
    samps, probes_n, samples,
    methyl, atlas, ids, scores, out,
    pmsg, prcv, gcol, dmsg, drcv, cmsg, crcv, lmsg, lrcv, resid, smsg, srcv, lsplit,
    nmsg, nrcv, near, znat, zall, pown, pfar, pin, amsg, ain, bsum, ymsg, yin, final, xmsg, xin,
    psem, prsem, dsem, drsem, csem, crsem, lsem, lrsem, ssem, srsem,
    nsem, nrsem, msem, mrsem, osem, orsem, zsem, zrsem, ysem, yrsem, xsem, xrsem,
):
    me_p = lax.axis_index("probe")
    me_s = lax.axis_index("samp")
    blocks, share, cols = methyl.shape
    rows = blocks * share
    width = cols // samps
    phases = share // GROUP
    core = lax.rem(me_p, 2)
    z_at = lax.rem(me_p // 2, 4)
    y_at = me_p // 8
    sibling = me_p + 1 - 2 * core
    partner = me_p + 8 - 16 * y_at
    ahead = lax.rem(me_s + 1, samps)
    behind = lax.rem(me_s + samps - 1, samps)

    barrier = pltpu.get_barrier_semaphore()

    def greet(axis, peers, me):
        def body(step, carry):
            pl.semaphore_signal(
                barrier, inc=1, device_id={axis: lax.rem(me + step, peers)}, device_id_type=MESH
            )
            return carry
        lax.fori_loop(1, peers, body, 0)

    def greet_diagonal(step, carry):
        other = lax.rem(me_p + step, probes_n)
        for side in (ahead, behind):
            pl.semaphore_signal(
                barrier, inc=1, device_id={"samp": side, "probe": other}, device_id_type=MESH
            )
        return carry
    greet("samp", samps, me_s)
    greet("probe", probes_n, me_p)
    lax.fori_loop(1, probes_n, greet_diagonal, 0)

    kinds = atlas.shape[0]
    select_t = (lax.broadcasted_iota(jnp.int32, (kinds, kinds), 0) == ids[...]).astype(F32)
    selector = select_t.T[:K].astype(BF16)
    panel = dot(selector, atlas[...]).astype(BF16)
    gram_part = dot(panel, panel, ((1,), (1,)))
    pad = jnp.zeros((K, 128 - share - K), F32)

    def project(step, carry):
        block = methyl[pl.ds(2 * step, 2)].reshape(2 * share, cols)
        part = dot(panel, block, ((1,), (1,)))
        pmsg[2 * step] = jnp.concatenate([part[:, :share], gram_part, pad], axis=1)
        pmsg[2 * step + 1] = jnp.concatenate([part[:, share:], gram_part, pad], axis=1)
        return carry
    lax.fori_loop(0, probes_n // 2, project, 0)

    pl.semaphore_wait(barrier, probes_n - 1 + samps - 1 + 2 * (probes_n - 1))
    from_p = lambda peer: pmsg.at[peer]
    exchange_start(from_p, prcv, psem, prsem, "probe", probes_n, me_p)

    def bulk(phase):
        return copy_to(
            methyl.at[:, pl.ds(pl.multiple_of(phase * GROUP, GROUP), GROUP), :],
            zall.at[phases + phase], msem.at[phase], mrsem.at[phase], "samp", ahead,
        )

    def bulk_start(phase, carry):
        bulk(phase).start()
        return carry
    lax.fori_loop(0, phases, bulk_start, 0)

    prcv[me_p] = pmsg[me_p]
    exchange_wait(from_p, prcv, psem, prsem, "probe", probes_n, me_p)
    total = prcv[0]
    for peer in range(1, probes_n):
        total = total + prcv[peer]
    gram = total[:, share:share + K]
    proj = total[:, :share]

    diag = lax.broadcasted_iota(jnp.int32, (K, K), 0) == lax.broadcasted_iota(jnp.int32, (K, K), 1)
    trace = jnp.sum(jnp.where(diag, gram, 0.0), axis=(0, 1), keepdims=True)
    rate = 1.0 / trace
    scaled = gram * rate
    half = K // 2
    left_k = lax.broadcasted_iota(jnp.int32, (K, 128), 1) < share
    for k in range(half):
        gcol[k] = jnp.where(
            left_k,
            jnp.broadcast_to(scaled[:, k:k + 1], (K, 128)),
            jnp.broadcast_to(scaled[:, half + k:half + k + 1], (K, 128)),
        )
    goal = jnp.concatenate([proj[:half], proj[half:]], axis=1) * rate
    left = lax.broadcasted_iota(jnp.int32, (half, 128), 1) < share

    def descend(step, state):
        sums = [None, None]
        for k in range(half):
            term = gcol[k] * jnp.broadcast_to(state[k:k + 1, :], (K, 128))
            sums[k % 2] = term if sums[k % 2] is None else sums[k % 2] + term
        acc = sums[0] + sums[1]
        keep = jnp.where(left, acc[:half], acc[half:])
        other = jnp.where(left, acc[half:], acc[:half])
        grad = keep + pltpu.roll(other, share, axis=1) - goal
        return jnp.maximum(state - grad, 0.0)
    state = lax.fori_loop(0, ITERS, descend, jnp.full((half, 128), 1.0 / K, F32))
    weights = jnp.concatenate([state[:, :share], state[:, share:]], axis=0)
    scores[...] = weights * float(K)

    four = jnp.concatenate([weights] * 4, axis=0)
    wide = jnp.concatenate([four, jnp.zeros((4 * K, 128 - share), F32)], axis=1)
    dmsg[...] = wide.T[:share].astype(BF16)
    from_d = lambda peer: dmsg
    exchange_start(from_d, drcv, dsem, drsem, "probe", probes_n, me_p)
    drcv[me_p] = dmsg[...]
    exchange_wait(from_d, drcv, dsem, drsem, "probe", probes_n, me_p)
    design4 = drcv[...].reshape(rows, 4 * K)
    design = design4.astype(F32).T[:K].astype(BF16)
    nmsg[...] = design
    to_next = copy_to(nmsg, nrcv, nsem, nrsem, "samp", ahead)
    to_next.start()

    wgram_part = dot(design, design, ((1,), (1,)))
    wpad = jnp.concatenate([wgram_part, jnp.zeros((K, 128 - K), F32)], axis=1)

    def crossing(step, carry):
        at = pl.ds(pl.multiple_of(step * width, width), width)
        cmsg[step] = jnp.concatenate([dot(design, methyl[:, :, at].reshape(rows, width)), wpad], axis=1)
        return carry
    lax.fori_loop(0, samps, crossing, 0)
    from_c = lambda peer: cmsg.at[peer]
    exchange_start(from_c, crcv, csem, crsem, "samp", samps, me_s)
    crcv[me_s] = cmsg[me_s]
    exchange_wait(from_c, crcv, csem, crsem, "samp", samps, me_s)
    both = crcv[0]
    for peer in range(1, samps):
        both = both + crcv[peer]

    matrix = both[:, width:]
    row_id = lax.broadcasted_iota(jnp.int32, (K, 128), 0)
    lane_id = lax.broadcasted_iota(jnp.int32, (K, 128), 1)
    matrix = matrix + jnp.where(row_id == lane_id, 0.0001 * samples, 0.0)
    right = both[:, :width]
    row_w = lax.broadcasted_iota(jnp.int32, (K, 1), 0)
    for k in range(K):
        column = matrix[:, k:k + 1]
        pivot = 1.0 / matrix[k:k + 1, k:k + 1]
        factor = jnp.where(row_w == k, 0.0, column * pivot)
        matrix_row = matrix[k:k + 1, :]
        right_row = right[k:k + 1, :]
        matrix = matrix - factor * matrix_row
        right = right - factor * right_row
    pivots = jnp.sum(jnp.where(row_id == lane_id, matrix, 0.0), axis=1, keepdims=True)
    lmsg[...] = right / pivots
    from_l = lambda peer: lmsg
    exchange_start(from_l, lrcv, lsem, lrsem, "samp", samps, me_s)
    lrcv[me_s] = lmsg[...]
    exchange_wait(from_l, lrcv, lsem, lrsem, "samp", samps, me_s)

    part_blocks = 256 // share

    def residue(step, carry):
        high, mid, low = split3(lrcv[step])
        stacked = jnp.concatenate([high, mid, low, jnp.zeros_like(low)], axis=0)
        at = pl.ds(pl.multiple_of(step * width, width), width)
        lsplit[:, at] = stacked
        sums = jnp.zeros((1, width), F32)
        for b in range(0, blocks, part_blocks):
            res = methyl[b:b + part_blocks, :, at].reshape(256, width).astype(F32) - dot(
                drcv[b:b + part_blocks].reshape(256, 4 * K), stacked
            )
            resid[b * share:b * share + 256, at] = res
            sums = sums + jnp.sum(res * res, axis=0, keepdims=True)
        smsg[:, at] = sums
        return carry
    lax.fori_loop(0, samps, residue, 0)
    from_s = lambda peer: smsg
    exchange_start(from_s, srcv, ssem, srsem, "samp", samps, me_s)
    srcv[me_s] = smsg[...]
    exchange_wait(from_s, srcv, ssem, srsem, "samp", samps, me_s)
    spread = srcv[0]
    for peer in range(1, samps):
        spread = spread + srcv[peer]
    smsg[...] = lax.rsqrt(spread * (1.0 / samples) + 1e-06)

    def normalize(step, carry):
        at = pl.ds(pl.multiple_of(step * width, width), width)
        for b in range(0, blocks, part_blocks):
            value = (resid[b * share:b * share + 256, at] * smsg[:, at]).astype(BF16)
            value = value.reshape(part_blocks, share, width)
            znat[b:b + part_blocks, :, at] = value
            for phase in range(phases):
                zall[phase, b:b + part_blocks, :, at] = value[:, phase * GROUP:(phase + 1) * GROUP]
        return carry
    lax.fori_loop(0, samps, normalize, 0)

    to_next.wait_recv()
    others = nrcv[...].astype(F32)
    near[...] = jnp.concatenate([others] * 4, axis=0).T.astype(BF16).reshape(blocks, share, 4 * K)

    unit_rows = blocks * GROUP

    def to_sibling(unit):
        return copy_to(pfar.at[unit], pin.at[unit], osem.at[unit], orsem.at[unit], "probe", sibling)

    def along_z(unit, step):
        z_to = lax.rem(z_at + step, 4)
        return copy_to(
            amsg.at[unit, z_to], ain.at[unit, step], zsem.at[unit, step], zrsem.at[unit, step],
            "probe", y_at * 8 + z_to * 2 + core,
        )

    def to_partner(unit):
        return copy_to(ymsg.at[unit], yin.at[unit], ysem.at[unit], yrsem.at[unit], "probe", partner)

    def to_behind(phase, other):
        return pltpu.make_async_remote_copy(
            src_ref=xmsg.at[phase, other], dst_ref=xin.at[me_p, phase],
            send_sem=xsem.at[phase, other], recv_sem=xrsem.at[phase, me_p],
            device_id={"samp": behind, "probe": other}, device_id_type=MESH,
        )

    def prepare(unit):
        phase = unit - phases
        bulk(phase).wait_recv()
        group = near[:, pl.ds(pl.multiple_of(phase * GROUP, GROUP), GROUP), :].reshape(unit_rows, 4 * K)

        def body(step, carry):
            at = pl.ds(pl.multiple_of(step * width, width), width)
            raw = zall[unit, :, :, at].reshape(unit_rows, width).astype(F32)
            value = (raw - dot(group, lsplit[:, at])) * smsg[:, at]
            zall[unit, :, :, at] = value.astype(BF16).reshape(blocks, GROUP, width)
            return carry
        lax.fori_loop(0, samps, body, 0)

    def multiply(unit):
        def body(step, carry):
            at = pl.ds(pl.multiple_of(step * 256, 256), 256)
            other = znat[pl.ds(step * part_blocks, part_blocks)].reshape(256, cols)
            part = dot(zall[unit].reshape(unit_rows, cols), other, ((1,), (1,)))
            part = part.reshape(blocks // 2, 2, GROUP, 256)
            mine = jnp.where(core == 0, part[:, 0], part[:, 1])
            far = jnp.where(core == 0, part[:, 1], part[:, 0])
            pown[unit, :, :, at] = mine
            pfar[unit, :, :, at] = far.astype(BF16)
            return carry
        lax.fori_loop(0, rows // 256, body, 0)
        to_sibling(unit).start()

    def sum_cores(unit):
        to_sibling(unit).wait_recv()
        for z in range(4):
            for y in range(2):
                both_cores = pown[unit, 4 * y + z] + pin[unit, 4 * y + z].astype(F32)
                pown[unit, 4 * y + z] = both_cores
                amsg[unit, z, y] = both_cores.astype(BF16)
        for step in range(1, 4):
            along_z(unit, step).start()

    def sum_z(unit):
        for step in range(1, 4):
            along_z(unit, step).wait_recv()
        for y in range(2):
            value = pown[unit, 4 * y + z_at]
            for step in range(1, 4):
                value = value + ain[unit, step, y].astype(F32)
            bsum[unit, y] = value
        ymsg[unit] = bsum[unit, 1 - y_at]
        to_partner(unit).start()

    def sum_y(unit):
        to_partner(unit).wait_recv()
        value = (bsum[unit, y_at] + yin[unit]) * (1.0 / (cols * probes_n))
        tile = unit // phases
        phase = unit - tile * phases
        final[tile, pl.ds(pl.multiple_of(phase * GROUP, GROUP), GROUP)] = value

        @pl.when(tile == 1)
        def _():
            for other in range(blocks):
                xmsg[phase, other] = value[:, other * share:(other + 1) * share]

            def send(other, carry):
                to_behind(phase, other).start()
                return carry
            lax.fori_loop(0, blocks, send, 0)

    units = 2 * phases
    last = units - 1

    def pipeline(unit, carry):
        @pl.when(unit >= phases)
        def _():
            prepare(unit)
        multiply(unit)

        @pl.when(unit >= 1)
        def _():
            sum_cores(unit - 1)

        @pl.when(unit >= 2)
        def _():
            sum_z(unit - 2)

        @pl.when(unit >= 3)
        def _():
            sum_y(unit - 3)
        return carry
    lax.fori_loop(0, last, pipeline, 0)
    sum_cores(last - 1)

    def drain(unit, carry):
        sum_z(unit)
        sum_y(unit - 1)
        return carry
    lax.fori_loop(last - 2, last, drain, 0)
    sum_y(last - 1)
    out[0] = final[0].T
    prepare(last)
    multiply(last)
    sum_cores(last)
    sum_z(last)
    sum_y(last)
    out[1] = final[1].T

    def receive(phase, carry):
        def body(other, inner):
            pltpu.make_async_remote_copy(
                src_ref=xmsg.at[phase, other], dst_ref=xin.at[other, phase],
                send_sem=xsem.at[phase, other], recv_sem=xrsem.at[phase, other],
                device_id={"samp": ahead, "probe": other}, device_id_type=MESH,
            ).wait_recv()
            return inner
        return lax.fori_loop(0, blocks, body, carry)
    lax.fori_loop(0, phases, receive, 0)
    out[2] = xin[...].reshape(rows, share)

    def sent(unit, carry):
        to_sibling(unit).wait_send()
        for step in range(1, 4):
            along_z(unit, step).wait_send()
        to_partner(unit).wait_send()
        return carry
    lax.fori_loop(0, units, sent, 0)

    def sent_out(phase, carry):
        bulk(phase).wait_send()

        def body(other, inner):
            to_behind(phase, other).wait_send()
            return inner
        return lax.fori_loop(0, blocks, body, carry)
    lax.fori_loop(0, phases, sent_out, 0)
    to_next.wait_send()


def whole(mesh, methyl, atlas, panel_ids):
    samps, probes_n = mesh.shape["samp"], mesh.shape["probe"]
    rows, cols = methyl.shape
    share, width = rows // probes_n, cols // samps
    phases = share // GROUP
    units = 2 * phases
    per_core = probes_n // 2
    vmem = pl.BlockSpec(memory_space=pltpu.VMEM)
    dma = pltpu.SemaphoreType.DMA
    return pl.pallas_call(
        functools.partial(program_kernel, samps, probes_n, rows * samps),
        out_shape=(
            jax.ShapeDtypeStruct((K, share), F32),
            jax.ShapeDtypeStruct((3, rows, share), F32),
        ),
        in_specs=[vmem] * 3,
        out_specs=(vmem,) * 2,
        scratch_shapes=[
            pltpu.VMEM((probes_n, K, 128), F32),
            pltpu.VMEM((probes_n, K, 128), F32),
            pltpu.VMEM((K // 2, K, 128), F32),
            pltpu.VMEM((share, 4 * K), BF16),
            pltpu.VMEM((probes_n, share, 4 * K), BF16),
            pltpu.VMEM((samps, K, width + 128), F32),
            pltpu.VMEM((samps, K, width + 128), F32),
            pltpu.VMEM((K, width), F32),
            pltpu.VMEM((samps, K, width), F32),
            pltpu.VMEM((rows, cols), F32),
            pltpu.VMEM((1, cols), F32),
            pltpu.VMEM((samps, 1, cols), F32),
            pltpu.VMEM((4 * K, cols), BF16),
            pltpu.VMEM((K, rows), BF16),
            pltpu.VMEM((K, rows), BF16),
            pltpu.VMEM((probes_n, share, 4 * K), BF16),
            pltpu.VMEM((probes_n, share, cols), BF16),
            pltpu.VMEM((units, probes_n, GROUP, cols), BF16),
            pltpu.VMEM((units, per_core, GROUP, rows), F32),
            pltpu.VMEM((units, per_core, GROUP, rows), BF16),
            pltpu.VMEM((units, per_core, GROUP, rows), BF16),
            pltpu.VMEM((units, 4, 2, GROUP, rows), BF16),
            pltpu.VMEM((units, 4, 2, GROUP, rows), BF16),
            pltpu.VMEM((units, 2, GROUP, rows), F32),
            pltpu.VMEM((units, GROUP, rows), F32),
            pltpu.VMEM((units, GROUP, rows), F32),
            pltpu.VMEM((2, share, rows), F32),
            pltpu.VMEM((phases, probes_n, GROUP, share), F32),
            pltpu.VMEM((probes_n, phases, GROUP, share), F32),
            dma((probes_n,)), dma((probes_n,)), dma((probes_n,)), dma((probes_n,)),
            dma((samps,)), dma((samps,)), dma((samps,)), dma((samps,)), dma((samps,)), dma((samps,)),
            dma, dma, dma((phases,)), dma((phases,)), dma((units,)), dma((units,)),
            dma((units, 4)), dma((units, 4)), dma((units,)), dma((units,)),
            dma((phases, probes_n)), dma((phases, probes_n)),
        ],
        compiler_params=pltpu.CompilerParams(
            collective_id=0, has_side_effects=True, vmem_limit_bytes=60 * 1024 * 1024
        ),
        name="whole",
    )(methyl.reshape(probes_n, share, cols), atlas, panel_ids.reshape(1, -1))


def solution(mesh):
    def body(methyl, atlas, panel_ids):
        scores, relmat = whole(mesh, methyl, atlas, panel_ids)
        return relmat, scores

    return jax.shard_map(
        body,
        mesh=mesh,
        in_specs=(P("samp", "probe"), P(None, "probe"), P()),
        out_specs=(P(None, "samp", "probe"), P(None, ("samp", "probe"))),
        check_vma=False,
    )
```

```python
import functools

import jax
import jax.numpy as jnp
from jax import lax
from jax.experimental import pallas as pl
from jax.experimental.pallas import tpu as pltpu
from jax.sharding import PartitionSpec as P

K = 32
ITERS = 128
GROUP = 16
PIECE = 4
BULK = (4, 5, 6, 7, 8)
RELAY = (0, 1, 2, 3, 4, 5, 6, 7)
EACH = 2
EACH_RELAY = 2
LAG_Z = 2
LAG_Y = 4
MESH = pl.DeviceIdType.MESH
F32 = jnp.float32
BF16 = jnp.bfloat16


def dot(a, b, dims=((1,), (0,))):
    return lax.dot_general(a, b, (dims, ((), ())), preferred_element_type=F32)


def copy_to(src, dst, send_sem, recv_sem, axis, peer):
    return pltpu.make_async_remote_copy(
        src_ref=src, dst_ref=dst, send_sem=send_sem, recv_sem=recv_sem,
        device_id={axis: peer}, device_id_type=MESH,
    )


def exchange_start(src_of, dst, send_sem, recv_sem, axis, peers, me):
    def body(step, carry):
        peer = lax.rem(me + step, peers)
        copy_to(src_of(peer), dst.at[me], send_sem.at[peer], recv_sem.at[me], axis, peer).start()
        return carry
    lax.fori_loop(1, peers, body, 0)


def exchange_wait(src_of, dst, send_sem, recv_sem, axis, peers, me):
    def body(step, carry):
        peer = lax.rem(me + step, peers)
        copy = copy_to(src_of(peer), dst.at[peer], send_sem.at[peer], recv_sem.at[peer], axis, peer)
        copy.wait_recv()
        copy.wait_send()
        return carry
    lax.fori_loop(1, peers, body, 0)


def split3(value):
    high = value.astype(BF16)
    rest = value - high.astype(F32)
    mid = rest.astype(BF16)
    low = (rest - mid.astype(F32)).astype(BF16)
    return high, mid, low


def program_kernel(
    samps, probes_n, samples,
    methyl, atlas, ids, scores, out,
    pmsg, prcv, gcol, dmsg, drcv, cmsg, crcv, lmsg, lrcv, resid, smsg, srcv, lsplit,
    nmsg, nrcv, near, znat, raw, pown, pfar, pin, amsg, ain, bsum, ymsg, yin, final, xmsg, xin,
    psem, prsem, dsem, drsem, csem, crsem, lsem, lrsem, ssem, srsem,
    nsem, nrsem, msem, mrsem, rsem, rrsem, osem, orsem, zsem, zrsem, ysem, yrsem, xsem, xrsem,
):
    me_p = lax.axis_index("probe")
    me_s = lax.axis_index("samp")
    blocks, share, cols = methyl.shape
    rows = blocks * share
    width = cols // samps
    phases = share // GROUP
    core = lax.rem(me_p, 2)
    z_at = lax.rem(me_p // 2, 4)
    y_at = me_p // 8
    sibling = me_p + 1 - 2 * core
    partner = me_p + 8 - 16 * y_at
    odd = lax.rem(me_s, 2)
    mate = me_s + 1 - 2 * odd
    cousin = lax.rem(me_s + samps - 1 + 2 * odd, samps)
    onward = lax.rem(me_s + samps + 2 - 4 * odd, samps)
    reach = cols // 2
    held = pl.ds(pl.multiple_of(odd * reach, reach), reach)
    given = pl.ds(pl.multiple_of((1 - odd) * reach, reach), reach)

    barrier = pltpu.get_barrier_semaphore()

    def greet(axis, peers, me):
        def body(step, carry):
            pl.semaphore_signal(
                barrier, inc=1, device_id={axis: lax.rem(me + step, peers)}, device_id_type=MESH
            )
            return carry
        lax.fori_loop(1, peers, body, 0)

    greet("samp", samps, me_s)
    greet("probe", probes_n, me_p)

    kinds = atlas.shape[0]
    select_t = (lax.broadcasted_iota(jnp.int32, (kinds, kinds), 0) == ids[...]).astype(F32)
    selector = select_t.T[:K].astype(BF16)
    panel = dot(selector, atlas[...]).astype(BF16)
    gram_part = dot(panel, panel, ((1,), (1,)))
    pad = jnp.zeros((K, 128 - share - K), F32)

    def project(step, carry):
        block = methyl[pl.ds(2 * step, 2)].reshape(2 * share, cols)
        part = dot(panel, block, ((1,), (1,)))
        pmsg[2 * step] = jnp.concatenate([part[:, :share], gram_part, pad], axis=1)
        pmsg[2 * step + 1] = jnp.concatenate([part[:, share:], gram_part, pad], axis=1)
        return carry
    lax.fori_loop(0, probes_n // 2, project, 0)

    pl.semaphore_wait(barrier, probes_n - 1 + samps - 1)
    from_p = lambda peer: pmsg.at[peer]
    exchange_start(from_p, prcv, psem, prsem, "probe", probes_n, me_p)

    parts = blocks // PIECE
    pieces = phases * parts

    def place(piece):
        phase = piece // parts
        return phase, pl.ds((piece - phase * parts) * PIECE, PIECE)

    def bulk(piece):
        phase, at = place(piece)
        return copy_to(
            methyl.at[at, pl.ds(pl.multiple_of(phase * GROUP, GROUP), GROUP), given],
            raw.at[0, phase, at], msem.at[piece], mrsem.at[piece], "samp", mate,
        )

    def relay(piece):
        phase, at = place(piece)
        return copy_to(
            raw.at[0, phase, at], raw.at[1, phase, at], rsem.at[piece], rrsem.at[piece], "samp", onward,
        )

    def bulk_start(first, past):
        def body(piece, carry):
            bulk(piece).start()
            return carry
        lax.fori_loop(first, past, body, 0)

    def relay_start(first, past):
        def body(piece, carry):
            bulk(piece).wait_recv()
            relay(piece).start()
            return carry
        lax.fori_loop(first, past, body, 0)

    prcv[me_p] = pmsg[me_p]
    exchange_wait(from_p, prcv, psem, prsem, "probe", probes_n, me_p)
    total = prcv[0]
    for peer in range(1, probes_n):
        total = total + prcv[peer]
    gram = total[:, share:share + K]
    proj = total[:, :share]

    diag = lax.broadcasted_iota(jnp.int32, (K, K), 0) == lax.broadcasted_iota(jnp.int32, (K, K), 1)
    trace = jnp.sum(jnp.where(diag, gram, 0.0), axis=(0, 1), keepdims=True)
    rate = 1.0 / trace
    scaled = gram * rate
    half = K // 2
    left_k = lax.broadcasted_iota(jnp.int32, (K, 128), 1) < share
    for k in range(half):
        gcol[k] = jnp.where(
            left_k,
            jnp.broadcast_to(scaled[:, k:k + 1], (K, 128)),
            jnp.broadcast_to(scaled[:, half + k:half + k + 1], (K, 128)),
        )
    goal = jnp.concatenate([proj[:half], proj[half:]], axis=1) * rate
    left = lax.broadcasted_iota(jnp.int32, (half, 128), 1) < share

    def descend(step, state):
        sums = [None, None]
        for k in range(half):
            term = gcol[k] * jnp.broadcast_to(state[k:k + 1, :], (K, 128))
            sums[k % 2] = term if sums[k % 2] is None else sums[k % 2] + term
        acc = sums[0] + sums[1]
        keep = jnp.where(left, acc[:half], acc[half:])
        other = jnp.where(left, acc[half:], acc[:half])
        grad = keep + pltpu.roll(other, share, axis=1) - goal
        return jnp.maximum(state - grad, 0.0)
    bulk_start(0, BULK[0])
    state = jnp.full((half, 128), 1.0 / K, F32)
    for segment in range(4):
        state = lax.fori_loop(0, ITERS // 4, descend, state)
        if segment:
            relay_start(RELAY[segment - 1], RELAY[segment])
    weights = jnp.concatenate([state[:, :share], state[:, share:]], axis=0)
    scores[...] = weights * float(K)

    four = jnp.concatenate([weights] * 4, axis=0)
    wide = jnp.concatenate([four, jnp.zeros((4 * K, 128 - share), F32)], axis=1)
    dmsg[...] = wide.T[:share].astype(BF16)
    from_d = lambda peer: dmsg
    exchange_start(from_d, drcv, dsem, drsem, "probe", probes_n, me_p)
    drcv[me_p] = dmsg[...]
    exchange_wait(from_d, drcv, dsem, drsem, "probe", probes_n, me_p)
    design4 = drcv[...].reshape(rows, 4 * K)
    design = design4.astype(F32).T[:K].astype(BF16)
    nmsg[...] = design

    def issue(slot):
        bulk_start(BULK[slot - 1], BULK[slot])
        relay_start(RELAY[slot + 2], RELAY[slot + 3])
    issue(1)

    wgram_part = dot(design, design, ((1,), (1,)))
    wpad = jnp.concatenate([wgram_part, jnp.zeros((K, 128 - K), F32)], axis=1)

    def crossing(step, carry):
        at = pl.ds(pl.multiple_of(step * width, width), width)
        cmsg[step] = jnp.concatenate([dot(design, methyl[:, :, at].reshape(rows, width)), wpad], axis=1)
        return carry
    lax.fori_loop(0, samps, crossing, 0)
    from_c = lambda peer: cmsg.at[peer]
    exchange_start(from_c, crcv, csem, crsem, "samp", samps, me_s)
    crcv[me_s] = cmsg[me_s]
    exchange_wait(from_c, crcv, csem, crsem, "samp", samps, me_s)
    issue(2)
    both = crcv[0]
    for peer in range(1, samps):
        both = both + crcv[peer]

    matrix = both[:, width:]
    row_id = lax.broadcasted_iota(jnp.int32, (K, 128), 0)
    lane_id = lax.broadcasted_iota(jnp.int32, (K, 128), 1)
    matrix = matrix + jnp.where(row_id == lane_id, 0.0001 * samples, 0.0)
    right = both[:, :width]
    row_w = lax.broadcasted_iota(jnp.int32, (K, 1), 0)
    for k in range(K):
        column = matrix[:, k:k + 1]
        pivot = 1.0 / matrix[k:k + 1, k:k + 1]
        factor = jnp.where(row_w == k, 0.0, column * pivot)
        matrix_row = matrix[k:k + 1, :]
        right_row = right[k:k + 1, :]
        matrix = matrix - factor * matrix_row
        right = right - factor * right_row
    pivots = jnp.sum(jnp.where(row_id == lane_id, matrix, 0.0), axis=1, keepdims=True)
    lmsg[...] = right / pivots
    from_l = lambda peer: lmsg
    exchange_start(from_l, lrcv, lsem, lrsem, "samp", samps, me_s)
    lrcv[me_s] = lmsg[...]
    exchange_wait(from_l, lrcv, lsem, lrsem, "samp", samps, me_s)

    issue(3)
    part_blocks = 256 // share

    def residue(step, carry):
        high, mid, low = split3(lrcv[step])
        stacked = jnp.concatenate([high, mid, low, jnp.zeros_like(low)], axis=0)
        at = pl.ds(pl.multiple_of(step * width, width), width)
        lsplit[:, at] = stacked
        sums = jnp.zeros((1, width), F32)
        for b in range(0, blocks, part_blocks):
            res = methyl[b:b + part_blocks, :, at].reshape(256, width).astype(F32) - dot(
                drcv[b:b + part_blocks].reshape(256, 4 * K), stacked
            )
            resid[b * share:b * share + 256, at] = res
            sums = sums + jnp.sum(res * res, axis=0, keepdims=True)
        smsg[:, at] = sums
        return carry
    lax.fori_loop(0, samps, residue, 0)
    from_s = lambda peer: smsg
    exchange_start(from_s, srcv, ssem, srsem, "samp", samps, me_s)
    srcv[me_s] = smsg[...]
    exchange_wait(from_s, srcv, ssem, srsem, "samp", samps, me_s)
    to_mate = copy_to(nmsg, nrcv.at[0], nsem.at[0], nrsem.at[0], "samp", mate)
    to_cousin = copy_to(nmsg, nrcv.at[1], nsem.at[1], nrsem.at[1], "samp", cousin)
    to_mate.start()
    to_cousin.start()
    issue(4)
    spread = srcv[0]
    for peer in range(1, samps):
        spread = spread + srcv[peer]
    smsg[...] = lax.rsqrt(spread * (1.0 / samples) + 1e-06)

    def normalize(step, carry):
        at = pl.ds(pl.multiple_of(step * width, width), width)
        for b in range(0, blocks, part_blocks):
            value = (resid[b * share:b * share + 256, at] * smsg[:, at]).astype(BF16)
            value = value.reshape(part_blocks, share, width)
            znat[b:b + part_blocks, :, at] = value
        return carry
    lax.fori_loop(0, samps, normalize, 0)

    def widen(which, copy):
        copy.wait_recv()
        others = nrcv[which].astype(F32)
        near[which] = jnp.concatenate([others] * 4, axis=0).T.astype(BF16).reshape(blocks, share, 4 * K)

    unit_rows = blocks * GROUP

    def to_sibling(unit):
        return copy_to(pfar.at[unit], pin.at[unit], osem.at[unit], orsem.at[unit], "probe", sibling)

    def along_z(unit, step):
        z_to = lax.rem(z_at + step, 4)
        return copy_to(
            amsg.at[unit, z_to], ain.at[unit, step], zsem.at[unit, step], zrsem.at[unit, step],
            "probe", y_at * 8 + z_to * 2 + core,
        )

    def to_partner(unit):
        return copy_to(ymsg.at[unit], yin.at[unit], ysem.at[unit], yrsem.at[unit], "probe", partner)

    def across(which, phase, other, slot):
        return pltpu.make_async_remote_copy(
            src_ref=xmsg.at[which, phase, other], dst_ref=xin.at[which, slot, phase],
            send_sem=xsem.at[which, phase, other], recv_sem=xrsem.at[which, phase, slot],
            device_id={"samp": jnp.where(which == 0, mate, cousin), "probe": other}, device_id_type=MESH,
        )

    def prepare(unit):
        which = unit // phases - 1
        phase = lax.rem(unit, phases)
        first, past = phase * parts, (phase + 1) * parts

        @pl.when(which == 1)
        def _():
            def arrive(piece, carry):
                relay(piece).wait_recv()
                return carry
            lax.fori_loop(first, past, arrive, 0)

        @pl.when(which == 0)
        def _():
            def depart(piece, carry):
                relay(piece).wait_send()
                return carry
            lax.fori_loop(first, past, depart, 0)
        group = near[which, :, pl.ds(pl.multiple_of(phase * GROUP, GROUP), GROUP), :].reshape(unit_rows, 4 * K)

        def body(step, carry):
            at = pl.ds(pl.multiple_of(step * width, width), width)
            there = pl.ds(pl.multiple_of(odd * reach + step * width, width), width)
            value = raw[which, phase, :, :, at].reshape(unit_rows, width).astype(F32)
            value = (value - dot(group, lsplit[:, there])) * smsg[:, there]
            raw[which, phase, :, :, at] = value.astype(BF16).reshape(blocks, GROUP, width)
            return carry
        lax.fori_loop(0, reach // width, body, 0)

    def put(unit, at, part):
        part = part.reshape(blocks // 2, 2, GROUP, 256)
        pown[unit, :, :, at] = jnp.where(core == 0, part[:, 0], part[:, 1])
        pfar[unit, :, :, at] = jnp.where(core == 0, part[:, 1], part[:, 0]).astype(BF16)

    def multiply(unit):
        phase = lax.rem(unit, phases)

        @pl.when(unit < phases)
        def _():
            def body(step, carry):
                group = znat[:, pl.ds(pl.multiple_of(phase * GROUP, GROUP), GROUP), :].reshape(unit_rows, cols)
                other = znat[pl.ds(step * part_blocks, part_blocks)].reshape(256, cols)
                put(unit, pl.ds(pl.multiple_of(step * 256, 256), 256), dot(group, other, ((1,), (1,))))
                return carry
            lax.fori_loop(0, rows // 256, body, 0)

        @pl.when(unit >= phases)
        def _():
            def body(step, carry):
                group = raw[unit // phases - 1, phase].reshape(unit_rows, reach)
                other = znat[pl.ds(step * part_blocks, part_blocks), :, held].reshape(256, reach)
                put(unit, pl.ds(pl.multiple_of(step * 256, 256), 256), dot(group, other, ((1,), (1,))))
                return carry
            lax.fori_loop(0, rows // 256, body, 0)
        to_sibling(unit).start()

    def sum_cores(unit):
        to_sibling(unit).wait_recv()
        for z in range(4):
            for y in range(2):
                both_cores = pown[unit, 4 * y + z] + pin[unit, 4 * y + z].astype(F32)
                pown[unit, 4 * y + z] = both_cores
                amsg[unit, z, y] = both_cores.astype(BF16)
        for step in range(1, 4):
            along_z(unit, step).start()

    def sum_z(unit):
        for step in range(1, 4):
            along_z(unit, step).wait_recv()
        for y in range(2):
            value = pown[unit, 4 * y + z_at]
            for step in range(1, 4):
                value = value + ain[unit, step, y].astype(F32)
            bsum[unit, y] = value
        ymsg[unit] = bsum[unit, 1 - y_at]
        to_partner(unit).start()

    def sum_y(unit):
        to_partner(unit).wait_recv()
        value = (bsum[unit, y_at] + yin[unit]) * (1.0 / (cols * probes_n))
        tile = unit // phases
        phase = unit - tile * phases
        final[tile, pl.ds(pl.multiple_of(phase * GROUP, GROUP), GROUP)] = value

        @pl.when(tile >= 1)
        def _():
            for other in range(blocks):
                xmsg[tile - 1, phase, other] = value[:, other * share:(other + 1) * share]

            def send(other, carry):
                across(tile - 1, phase, other, me_p).start()
                return carry
            lax.fori_loop(0, blocks, send, 0)

    units = 3 * phases

    def pipeline(unit, carry):
        bulk_start(
            jnp.minimum(BULK[4] + unit * EACH, pieces), jnp.minimum(BULK[4] + unit * EACH + EACH, pieces)
        )

        @pl.when(unit == phases)
        def _():
            widen(0, to_mate)

        @pl.when(unit == 2 * phases)
        def _():
            widen(1, to_cousin)

        @pl.when(jnp.logical_and(unit >= phases, unit < units))
        def _():
            prepare(unit)

        @pl.when(unit < units)
        def _():
            multiply(unit)

        @pl.when(jnp.logical_and(unit >= 1, unit < units + 1))
        def _():
            sum_cores(unit - 1)

        @pl.when(jnp.logical_and(unit >= LAG_Z, unit < units + LAG_Z))
        def _():
            sum_z(unit - LAG_Z)

        @pl.when(unit >= LAG_Y)
        def _():
            sum_y(unit - LAG_Y)
        relay_start(
            jnp.minimum(RELAY[7] + unit * EACH_RELAY, pieces),
            jnp.minimum(RELAY[7] + unit * EACH_RELAY + EACH_RELAY, pieces),
        )
        return carry
    lax.fori_loop(0, units + LAG_Y, pipeline, 0)
    out[0] = final[0]

    def receive(phase, carry):
        def body(other, inner):
            across(0, phase, other, other).wait_recv()
            across(1, phase, other, other).wait_recv()
            return inner
        return lax.fori_loop(0, blocks, body, carry)
    lax.fori_loop(0, phases, receive, 0)
    out[2 - odd] = final[1] + xin[0].reshape(rows, share).T
    out[1 + odd] = final[2] + xin[1].reshape(rows, share).T

    def sent(unit, carry):
        to_sibling(unit).wait_send()
        for step in range(1, 4):
            along_z(unit, step).wait_send()
        to_partner(unit).wait_send()
        return carry
    lax.fori_loop(0, units, sent, 0)

    def sent_out(phase, carry):
        def leave(piece, inner):
            bulk(piece).wait_send()
            return inner
        lax.fori_loop(phase * parts, (phase + 1) * parts, leave, 0)

        def body(other, inner):
            across(0, phase, other, me_p).wait_send()
            across(1, phase, other, me_p).wait_send()
            return inner
        return lax.fori_loop(0, blocks, body, carry)
    lax.fori_loop(0, phases, sent_out, 0)
    to_mate.wait_send()
    to_cousin.wait_send()


def whole(mesh, methyl, atlas, panel_ids):
    samps, probes_n = mesh.shape["samp"], mesh.shape["probe"]
    rows, cols = methyl.shape
    share, width = rows // probes_n, cols // samps
    phases = share // GROUP
    units = 3 * phases
    pieces = phases * (probes_n // PIECE)
    per_core = probes_n // 2
    vmem = pl.BlockSpec(memory_space=pltpu.VMEM)
    dma = pltpu.SemaphoreType.DMA
    return pl.pallas_call(
        functools.partial(program_kernel, samps, probes_n, rows * samps),
        out_shape=(
            jax.ShapeDtypeStruct((K, share), F32),
            jax.ShapeDtypeStruct((3, share, rows), F32),
        ),
        in_specs=[vmem] * 3,
        out_specs=(vmem,) * 2,
        scratch_shapes=[
            pltpu.VMEM((probes_n, K, 128), F32),
            pltpu.VMEM((probes_n, K, 128), F32),
            pltpu.VMEM((K // 2, K, 128), F32),
            pltpu.VMEM((share, 4 * K), BF16),
            pltpu.VMEM((probes_n, share, 4 * K), BF16),
            pltpu.VMEM((samps, K, width + 128), F32),
            pltpu.VMEM((samps, K, width + 128), F32),
            pltpu.VMEM((K, width), F32),
            pltpu.VMEM((samps, K, width), F32),
            pltpu.VMEM((rows, cols), F32),
            pltpu.VMEM((1, cols), F32),
            pltpu.VMEM((samps, 1, cols), F32),
            pltpu.VMEM((4 * K, cols), BF16),
            pltpu.VMEM((K, rows), BF16),
            pltpu.VMEM((2, K, rows), BF16),
            pltpu.VMEM((2, probes_n, share, 4 * K), BF16),
            pltpu.VMEM((probes_n, share, cols), BF16),
            pltpu.VMEM((2, phases, probes_n, GROUP, cols // 2), BF16),
            pltpu.VMEM((units, per_core, GROUP, rows), F32),
            pltpu.VMEM((units, per_core, GROUP, rows), BF16),
            pltpu.VMEM((units, per_core, GROUP, rows), BF16),
            pltpu.VMEM((units, 4, 2, GROUP, rows), BF16),
            pltpu.VMEM((units, 4, 2, GROUP, rows), BF16),
            pltpu.VMEM((units, 2, GROUP, rows), F32),
            pltpu.VMEM((units, GROUP, rows), F32),
            pltpu.VMEM((units, GROUP, rows), F32),
            pltpu.VMEM((3, share, rows), F32),
            pltpu.VMEM((2, phases, probes_n, GROUP, share), F32),
            pltpu.VMEM((2, probes_n, phases, GROUP, share), F32),
            dma((probes_n,)), dma((probes_n,)), dma((probes_n,)), dma((probes_n,)),
            dma((samps,)), dma((samps,)), dma((samps,)), dma((samps,)), dma((samps,)), dma((samps,)),
            dma((2,)), dma((2,)), dma((pieces,)), dma((pieces,)), dma((pieces,)), dma((pieces,)), dma((units,)), dma((units,)),
            dma((units, 4)), dma((units, 4)), dma((units,)), dma((units,)),
            dma((2, phases, probes_n)), dma((2, phases, probes_n)),
        ],
        compiler_params=pltpu.CompilerParams(
            collective_id=0, has_side_effects=True, vmem_limit_bytes=60 * 1024 * 1024
        ),
        name="whole",
    )(methyl.reshape(probes_n, share, cols), atlas, panel_ids.reshape(1, -1))


def solution(mesh):
    def body(methyl, atlas, panel_ids):
        scores, relmat = whole(mesh, methyl, atlas, panel_ids)
        return jnp.swapaxes(relmat, 1, 2), scores

    return jax.shard_map(
        body,
        mesh=mesh,
        in_specs=(P("samp", "probe"), P(None, "probe"), P()),
        out_specs=(P(None, "samp", "probe"), P(None, ("samp", "probe"))),
        check_vma=False,
    )
```

```python
import functools

import jax
import jax.numpy as jnp
from jax import lax
from jax.experimental import pallas as pl
from jax.experimental.pallas import tpu as pltpu
from jax.sharding import PartitionSpec as P

K = 32
ITERS = 128
GROUP = 16
PIECE = 4
BULK = (3, 4, 5, 6, 8)
RELAY = (0, 0, 0, 1, 2, 3, 4, 5)
EACH = 2
PACE = 2
LAGS = (1, 3, 5, 7, 9)
ORDER = (0, 1, 2, 4, 3, 5, 6, 7, 8, 9, 10, 11)
MESH = pl.DeviceIdType.MESH
F32 = jnp.float32
BF16 = jnp.bfloat16


def dot(a, b, dims=((1,), (0,))):
    return lax.dot_general(a, b, (dims, ((), ())), preferred_element_type=F32)


def copy_to(src, dst, send_sem, recv_sem, axis, peer):
    return pltpu.make_async_remote_copy(
        src_ref=src, dst_ref=dst, send_sem=send_sem, recv_sem=recv_sem,
        device_id={axis: peer}, device_id_type=MESH,
    )


def exchange_start(src_of, dst, send_sem, recv_sem, axis, peers, me):
    def body(step, carry):
        peer = lax.rem(me + step, peers)
        copy_to(src_of(peer), dst.at[me], send_sem, recv_sem, axis, peer).start()
        return carry
    lax.fori_loop(1, peers, body, 0)


def exchange_wait(dst, send_sem, recv_sem, axis, peers, me):
    rest = dst.at[pl.ds(0, peers - 1)]
    copy = copy_to(rest, rest, send_sem, recv_sem, axis, lax.rem(me + 1, peers))
    copy.wait_recv()
    copy.wait_send()


def split3(value):
    high = value.astype(BF16)
    rest = value - high.astype(F32)
    mid = rest.astype(BF16)
    low = (rest - mid.astype(F32)).astype(BF16)
    return high, mid, low


def program_kernel(
    samps, probes_n, samples,
    methyl, atlas, ids, scores, out,
    pmsg, prcv, gcol, dmsg, drcv, cmsg, crcv, lmsg, lrcv, resid, smsg, srcv, lsplit,
    nmsg, nrcv, near, znat, raw, pown, pfar, pin, amsg, ain, fmsg, fin, bsum, ymsg, yin, final, xin, sin,
    psem, prsem, dsem, drsem, csem, crsem, lsem, lrsem, ssem, srsem,
    nsem, nrsem, msem, mrsem, rsem, rrsem, osem, orsem, zsem, zrsem, fsem, frsem, ysem, yrsem, xsem, xrsem, wsem, wrsem,
):
    me_p = lax.axis_index("probe")
    me_s = lax.axis_index("samp")
    blocks, share, cols = methyl.shape
    rows = blocks * share
    width = cols // samps
    phases = share // GROUP
    core = lax.rem(me_p, 2)
    z_at = lax.rem(me_p // 2, 4)
    y_at = me_p // 8
    sibling = me_p + 1 - 2 * core
    partner = me_p + 8 - 16 * y_at
    odd = lax.rem(me_s, 2)
    mate = me_s + 1 - 2 * odd
    cousin = lax.rem(me_s + samps - 1 + 2 * odd, samps)
    onward = lax.rem(me_s + samps + 2 - 4 * odd, samps)
    reach = cols // 2
    held = pl.ds(pl.multiple_of(odd * reach, reach), reach)
    given = pl.ds(pl.multiple_of((1 - odd) * reach, reach), reach)

    barrier = pltpu.get_barrier_semaphore()

    def greet(axis, peers, me):
        def body(step, carry):
            pl.semaphore_signal(
                barrier, inc=1, device_id={axis: lax.rem(me + step, peers)}, device_id_type=MESH
            )
            return carry
        lax.fori_loop(1, peers, body, 0)

    greet("samp", samps, me_s)
    greet("probe", probes_n, me_p)

    kinds = atlas.shape[0]
    select_t = (lax.broadcasted_iota(jnp.int32, (kinds, kinds), 0) == ids[...]).astype(F32)
    selector = select_t.T[:K].astype(BF16)
    panel = dot(selector, atlas[...]).astype(BF16)
    gram_part = dot(panel, panel, ((1,), (1,)))
    pad = jnp.zeros((K, 128 - share - K), F32)

    def project(step, carry):
        block = methyl[pl.ds(2 * step, 2)].reshape(2 * share, cols)
        part = dot(panel, block, ((1,), (1,)))
        pmsg[2 * step] = jnp.concatenate([part[:, :share], gram_part, pad], axis=1)
        pmsg[2 * step + 1] = jnp.concatenate([part[:, share:], gram_part, pad], axis=1)
        return carry
    lax.fori_loop(0, probes_n // 2, project, 0)

    pl.semaphore_wait(barrier, probes_n - 1 + samps - 1)
    from_p = lambda peer: pmsg.at[peer]
    exchange_start(from_p, prcv, psem, prsem, "probe", probes_n, me_p)

    parts = blocks // PIECE
    pieces = phases * parts

    def place(piece):
        phase = piece // parts
        return phase, pl.ds((piece - phase * parts) * PIECE, PIECE)

    def bulk(piece):
        phase, at = place(piece)
        return copy_to(
            methyl.at[at, pl.ds(pl.multiple_of(phase * GROUP, GROUP), GROUP), given],
            raw.at[0, phase, at], msem, mrsem.at[piece], "samp", mate,
        )

    def relay(piece):
        phase, at = place(piece)
        return copy_to(
            raw.at[0, phase, at], raw.at[1, phase, at], rsem.at[piece], rrsem.at[piece], "samp", onward,
        )

    def bulk_start(first, past):
        def body(piece, carry):
            bulk(piece).start()
            return carry
        lax.fori_loop(first, past, body, 0)

    def relay_start(first, past):
        def body(piece, carry):
            bulk(piece).wait_recv()
            relay(piece).start()
            return carry
        lax.fori_loop(first, past, body, 0)

    prcv[me_p] = pmsg[me_p]
    exchange_wait(prcv, psem, prsem, "probe", probes_n, me_p)
    total = prcv[0]
    for peer in range(1, probes_n):
        total = total + prcv[peer]
    gram = total[:, share:share + K]

    diag = lax.broadcasted_iota(jnp.int32, (K, K), 0) == lax.broadcasted_iota(jnp.int32, (K, K), 1)
    trace = jnp.sum(jnp.where(diag, gram, 0.0), axis=(0, 1), keepdims=True)
    rate = 1.0 / trace
    moving = jnp.where(diag, 1.0, 0.0) - gram * rate
    for k in range(K):
        gcol[k] = jnp.broadcast_to(moving[:, k:k + 1], (K, 128))
    goal = total * rate

    def descend(step, state):
        sums = [goal, None]
        for k in range(K):
            term = gcol[k] * jnp.broadcast_to(state[k:k + 1, :], (K, 128))
            sums[k % 2] = term if sums[k % 2] is None else sums[k % 2] + term
        return jnp.maximum(sums[0] + sums[1], 0.0)
    bulk_start(0, BULK[0])
    state = jnp.full((K, 128), 1.0 / K, F32)
    for segment in range(4):
        state = lax.fori_loop(0, ITERS // 4, descend, state)
        if segment:
            relay_start(RELAY[segment - 1], RELAY[segment])
    weights = state[:, :share]
    scores[...] = weights * float(K)

    four = jnp.concatenate([weights] * 4, axis=0)
    wide = jnp.concatenate([four, jnp.zeros((4 * K, 128 - share), F32)], axis=1)
    dmsg[...] = wide.T[:share].astype(BF16)
    from_d = lambda peer: dmsg
    exchange_start(from_d, drcv, dsem, drsem, "probe", probes_n, me_p)
    drcv[me_p] = dmsg[...]
    exchange_wait(drcv, dsem, drsem, "probe", probes_n, me_p)
    design4 = drcv[...].reshape(rows, 4 * K)
    design = design4.astype(F32).T[:K].astype(BF16)
    nmsg[...] = design

    def issue(slot):
        bulk_start(BULK[slot - 1], BULK[slot])
        relay_start(RELAY[slot + 2], RELAY[slot + 3])
    issue(1)

    wgram_part = dot(design, design, ((1,), (1,)))
    wpad = jnp.concatenate([wgram_part, jnp.zeros((K, 128 - K), F32)], axis=1)

    def crossing(step, carry):
        at = pl.ds(pl.multiple_of(step * width, width), width)
        cmsg[step] = jnp.concatenate([dot(design, methyl[:, :, at].reshape(rows, width)), wpad], axis=1)
        return carry
    lax.fori_loop(0, samps, crossing, 0)
    from_c = lambda peer: cmsg.at[peer]
    exchange_start(from_c, crcv, csem, crsem, "samp", samps, me_s)
    crcv[me_s] = cmsg[me_s]
    exchange_wait(crcv, csem, crsem, "samp", samps, me_s)
    issue(2)
    both = crcv[0]
    for peer in range(1, samps):
        both = both + crcv[peer]

    matrix = both[:, width:]
    row_id = lax.broadcasted_iota(jnp.int32, (K, 128), 0)
    lane_id = lax.broadcasted_iota(jnp.int32, (K, 128), 1)
    matrix = matrix + jnp.where(row_id == lane_id, 0.0001 * samples, 0.0)
    right = both[:, :width]
    row_w = lax.broadcasted_iota(jnp.int32, (K, 1), 0)
    for k in range(K):
        column = matrix[:, k:k + 1]
        pivot = 1.0 / matrix[k:k + 1, k:k + 1]
        factor = jnp.where(row_w == k, 0.0, column * pivot)
        matrix_row = matrix[k:k + 1, :]
        right_row = right[k:k + 1, :]
        matrix = matrix - factor * matrix_row
        right = right - factor * right_row
    pivots = jnp.sum(jnp.where(row_id == lane_id, matrix, 0.0), axis=1, keepdims=True)
    lmsg[...] = right / pivots
    from_l = lambda peer: lmsg
    exchange_start(from_l, lrcv, lsem, lrsem, "samp", samps, me_s)
    lrcv[me_s] = lmsg[...]
    exchange_wait(lrcv, lsem, lrsem, "samp", samps, me_s)

    issue(3)
    part_blocks = 256 // share

    def residue(step, carry):
        high, mid, low = split3(lrcv[step])
        stacked = jnp.concatenate([high, mid, low, jnp.zeros_like(low)], axis=0)
        at = pl.ds(pl.multiple_of(step * width, width), width)
        lsplit[:, at] = stacked
        sums = jnp.zeros((1, width), F32)
        for b in range(0, blocks, part_blocks):
            res = methyl[b:b + part_blocks, :, at].reshape(256, width).astype(F32) - dot(
                drcv[b:b + part_blocks].reshape(256, 4 * K), stacked
            )
            resid[b * share:b * share + 256, at] = res
            sums = sums + jnp.sum(res * res, axis=0, keepdims=True)
        smsg[:, at] = sums
        return carry
    lax.fori_loop(0, samps, residue, 0)
    from_s = lambda peer: smsg
    exchange_start(from_s, srcv, ssem, srsem, "samp", samps, me_s)
    srcv[me_s] = smsg[...]
    exchange_wait(srcv, ssem, srsem, "samp", samps, me_s)
    to_mate = copy_to(nmsg, nrcv.at[0], nsem.at[0], nrsem.at[0], "samp", mate)
    to_cousin = copy_to(nmsg, nrcv.at[1], nsem.at[1], nrsem.at[1], "samp", cousin)
    to_mate.start()
    to_cousin.start()
    issue(4)
    spread = srcv[0]
    for peer in range(1, samps):
        spread = spread + srcv[peer]
    smsg[...] = lax.rsqrt(spread * (1.0 / samples) + 1e-06)

    def normalize(step, carry):
        at = pl.ds(pl.multiple_of(step * width, width), width)
        for b in range(0, blocks, part_blocks):
            value = (resid[b * share:b * share + 256, at] * smsg[:, at]).astype(BF16)
            value = value.reshape(part_blocks, share, width)
            znat[b:b + part_blocks, :, at] = value
        return carry
    lax.fori_loop(0, samps, normalize, 0)

    def widen(which, copy):
        copy.wait_recv()
        others = nrcv[which].astype(F32)
        near[which] = jnp.concatenate([others] * 4, axis=0).T.astype(BF16).reshape(blocks, share, 4 * K)

    unit_rows = blocks * GROUP

    def to_sibling(unit):
        return copy_to(pfar.at[unit], pin.at[unit], osem, orsem.at[unit], "probe", sibling)

    def along_z(unit, way):
        z_to = lax.rem(z_at + 1 + 2 * way, 4)
        return copy_to(
            amsg.at[unit, way], ain.at[unit, way], zsem, zrsem.at[unit],
            "probe", y_at * 8 + z_to * 2 + core,
        )

    def far_z(unit, way):
        z_to = lax.rem(z_at + 1 + 2 * way, 4)
        return copy_to(
            fmsg.at[unit, way], fin.at[unit, way], fsem, frsem.at[unit],
            "probe", y_at * 8 + z_to * 2 + core,
        )

    def to_partner(unit):
        return copy_to(ymsg.at[unit], yin.at[unit], ysem, yrsem.at[unit], "probe", partner)

    pair = 2 * GROUP
    mine = me_p // 2

    def across(which, part, chip):
        return pltpu.make_async_remote_copy(
            src_ref=final.at[1 + which, pl.ds(part * pair, pair), pl.ds(pl.multiple_of(chip * 128, 128), 128)],
            dst_ref=xin.at[which, part, mine],
            send_sem=xsem, recv_sem=xrsem.at[which, part],
            device_id={"samp": (mate, cousin)[which], "probe": 2 * chip + core}, device_id_type=MESH,
        )

    def swap(which, part):
        return copy_to(xin.at[which, part], sin.at[which, part], wsem, wrsem.at[which, part], "probe", sibling)

    def arrived(src, dst, send_sem, recv_sem):
        return copy_to(src, dst, send_sem, recv_sem, "probe", sibling)

    def prepare(unit):
        which, phase = unit // phases - 1, unit % phases
        for piece in range(phase * parts, (phase + 1) * parts):
            if which:
                relay(piece).wait_recv()
            else:
                relay(piece).wait_send()
        group = near[which, :, pl.ds(pl.multiple_of(phase * GROUP, GROUP), GROUP), :].reshape(unit_rows, 4 * K)

        def body(step, carry):
            at = pl.ds(pl.multiple_of(step * width, width), width)
            there = pl.ds(pl.multiple_of(odd * reach + step * width, width), width)
            value = raw[which, phase, :, :, at].reshape(unit_rows, width).astype(F32)
            value = (value - dot(group, lsplit[:, there])) * smsg[:, there]
            raw[which, phase, :, :, at] = value.astype(BF16).reshape(blocks, GROUP, width)
            return carry
        lax.fori_loop(0, reach // width, body, 0)

    def put(unit, at, part):
        part = part.reshape(blocks // 2, 2, GROUP, 256)
        pown[unit, :, :, at] = jnp.where(core == 0, part[:, 0], part[:, 1])
        pfar[unit, :, :, at] = jnp.where(core == 0, part[:, 1], part[:, 0]).astype(BF16)

    def multiply(unit):
        which, phase = unit // phases - 1, unit % phases

        def body(step, carry):
            theirs = pl.ds(step * part_blocks, part_blocks)
            if unit < phases:
                group = znat[:, phase * GROUP:(phase + 1) * GROUP, :].reshape(unit_rows, cols)
                other = znat[theirs].reshape(256, cols)
            else:
                group = raw[which, phase].reshape(unit_rows, reach)
                other = znat[theirs, :, held].reshape(256, reach)
            put(unit, pl.ds(pl.multiple_of(step * 256, 256), 256), dot(group, other, ((1,), (1,))))
            return carry
        lax.fori_loop(0, rows // 256, body, 0)
        to_sibling(unit).start()

    def sum_cores(unit):
        to_sibling(unit).wait_recv()
        for block in range(blocks // 2):
            pown[unit, block] = pown[unit, block] + pin[unit, block].astype(F32)
        across_z = lax.rem(z_at + 2, 4)
        for way in range(2):
            fmsg[unit, way] = pown[unit, 4 * way + across_z].astype(BF16)
            far_z(unit, way).start()

    def sum_far(unit):
        arrived(fmsg.at[unit], fin.at[unit], fsem, frsem.at[unit]).wait_recv()
        for way in range(2):
            z_to = lax.rem(z_at + 1 + 2 * way, 4)
            amsg[unit, way, way] = (pown[unit, 4 * way + z_to] + fin[unit, way].astype(F32)).astype(BF16)
            amsg[unit, way, 1 - way] = pown[unit, 4 * (1 - way) + z_to].astype(BF16)
            along_z(unit, way).start()

    def sum_z(unit):
        arrived(amsg.at[unit], ain.at[unit], zsem, zrsem.at[unit]).wait_recv()
        for y in range(2):
            bsum[unit, y] = (
                pown[unit, 4 * y + z_at] + ain[unit, 0, y].astype(F32) + ain[unit, 1, y].astype(F32)
            )
        ymsg[unit] = bsum[unit, 1 - y_at].astype(BF16)
        to_partner(unit).start()

    def sum_y(unit):
        to_partner(unit).wait_recv()
        value = (bsum[unit, y_at] + yin[unit].astype(F32)) * (1.0 / (cols * probes_n))
        tile, phase = divmod(unit, phases)
        final[tile, phase * GROUP:(phase + 1) * GROUP] = value
        if tile and phase % 2:
            def send(step, carry):
                across(tile - 1, phase // 2, lax.rem(mine + step, blocks // 2)).start()
                return carry
            lax.fori_loop(0, blocks // 2, send, 0)

    def pass_on(unit):
        tile, phase = divmod(unit, phases)
        if tile and phase % 2:
            which, part = tile - 1, phase // 2
            arrived(xin.at[which, part], xin.at[which, part], xsem, xrsem.at[which, part]).wait_recv()
            swap(which, part).start()

    units = 3 * phases

    bulk_done, relay_done = BULK[4], RELAY[7]
    for turn in range(units + LAGS[4]):
        more = min(bulk_done + EACH, pieces)
        bulk_start(bulk_done, more)
        bulk_done = more
        if turn < units:
            unit = ORDER[turn]
            if unit in (phases, 2 * phases):
                widen(*((0, to_mate) if unit == phases else (1, to_cousin)))
            if phases <= unit < 2 * phases:
                more = max(relay_done, (unit - phases + 1) * parts)
                relay_start(relay_done, more)
                relay_done = more
            if unit >= phases:
                prepare(unit)
            multiply(unit)
        for lag, stage in zip(LAGS, (sum_cores, sum_far, sum_z, sum_y, pass_on)):
            if 0 <= turn - lag < units:
                stage(ORDER[turn - lag])
        more = min(max(relay_done, RELAY[7] + int(PACE * (turn + 1))), bulk_done)
        relay_start(relay_done, more)
        relay_done = more
    out[0] = final[0]

    for which in range(2):
        for part in range(phases // 2):
            swap(which, part).wait_recv()
        for chip in range(blocks // 2):
            own, far = (
                jnp.concatenate([ref[which, part, chip] for part in range(phases // 2)], axis=0)
                for ref in (xin, sin)
            )
            rows_of_chip = jnp.concatenate(
                [jnp.where(core == 0, own, far), jnp.where(core == 0, far, own)], axis=0
            ).T
            at = slice(128 * chip, 128 * chip + 128)
            out[(2 - odd) if which == 0 else (1 + odd), :, at] = final[1 + which, :, at] + jnp.where(
                core == 0, rows_of_chip[:share], rows_of_chip[share:]
            )

    arrived(pfar, pin, osem, orsem.at[0]).wait_send()
    arrived(amsg, ain, zsem, zrsem.at[0]).wait_send()
    arrived(fmsg, fin, fsem, frsem.at[0]).wait_send()
    arrived(ymsg, yin, ysem, yrsem.at[0]).wait_send()
    arrived(xin, sin, xsem, wrsem.at[0, 0]).wait_send()
    arrived(xin, sin, wsem, wrsem.at[0, 0]).wait_send()
    arrived(raw.at[0], raw.at[1], msem, mrsem.at[0]).wait_send()
    to_mate.wait_send()
    to_cousin.wait_send()


def whole(mesh, methyl, atlas, panel_ids):
    samps, probes_n = mesh.shape["samp"], mesh.shape["probe"]
    rows, cols = methyl.shape
    share, width = rows // probes_n, cols // samps
    phases = share // GROUP
    units = 3 * phases
    pieces = phases * (probes_n // PIECE)
    per_core = probes_n // 2
    vmem = pl.BlockSpec(memory_space=pltpu.VMEM)
    dma = pltpu.SemaphoreType.DMA
    return pl.pallas_call(
        functools.partial(program_kernel, samps, probes_n, rows * samps),
        out_shape=(
            jax.ShapeDtypeStruct((K, share), F32),
            jax.ShapeDtypeStruct((3, share, rows), F32),
        ),
        in_specs=[vmem] * 3,
        out_specs=(vmem,) * 2,
        scratch_shapes=[
            pltpu.VMEM((probes_n, K, 128), F32),
            pltpu.VMEM((probes_n, K, 128), F32),
            pltpu.VMEM((K, K, 128), F32),
            pltpu.VMEM((share, 4 * K), BF16),
            pltpu.VMEM((probes_n, share, 4 * K), BF16),
            pltpu.VMEM((samps, K, width + 128), F32),
            pltpu.VMEM((samps, K, width + 128), F32),
            pltpu.VMEM((K, width), F32),
            pltpu.VMEM((samps, K, width), F32),
            pltpu.VMEM((rows, cols), F32),
            pltpu.VMEM((1, cols), F32),
            pltpu.VMEM((samps, 1, cols), F32),
            pltpu.VMEM((4 * K, cols), BF16),
            pltpu.VMEM((K, rows), BF16),
            pltpu.VMEM((2, K, rows), BF16),
            pltpu.VMEM((2, probes_n, share, 4 * K), BF16),
            pltpu.VMEM((probes_n, share, cols), BF16),
            pltpu.VMEM((2, phases, probes_n, GROUP, cols // 2), BF16),
            pltpu.VMEM((units, per_core, GROUP, rows), F32),
            pltpu.VMEM((units, per_core, GROUP, rows), BF16),
            pltpu.VMEM((units, per_core, GROUP, rows), BF16),
            pltpu.VMEM((units, 2, 2, GROUP, rows), BF16),
            pltpu.VMEM((units, 2, 2, GROUP, rows), BF16),
            pltpu.VMEM((units, 2, GROUP, rows), BF16),
            pltpu.VMEM((units, 2, GROUP, rows), BF16),
            pltpu.VMEM((units, 2, GROUP, rows), F32),
            pltpu.VMEM((units, GROUP, rows), BF16),
            pltpu.VMEM((units, GROUP, rows), BF16),
            pltpu.VMEM((3, share, rows), F32),
            pltpu.VMEM((2, phases // 2, per_core, 2 * GROUP, 2 * share), F32),
            pltpu.VMEM((2, phases // 2, per_core, 2 * GROUP, 2 * share), F32),
            dma, dma, dma, dma, dma, dma, dma, dma, dma, dma,
            dma((2,)), dma((2,)), dma, dma((pieces,)), dma((pieces,)), dma((pieces,)),
            dma, dma((units,)), dma, dma((units,)), dma, dma((units,)), dma, dma((units,)),
            dma, dma((2, phases // 2)), dma, dma((2, phases // 2)),
        ],
        compiler_params=pltpu.CompilerParams(
            collective_id=0, has_side_effects=True, vmem_limit_bytes=60 * 1024 * 1024
        ),
        name="whole",
    )(methyl.reshape(probes_n, share, cols), atlas, panel_ids.reshape(1, -1))


def solution(mesh):
    def body(methyl, atlas, panel_ids):
        scores, relmat = whole(mesh, methyl, atlas, panel_ids)
        return jnp.swapaxes(relmat, 1, 2), scores

    return jax.shard_map(
        body,
        mesh=mesh,
        in_specs=(P("samp", "probe"), P(None, "probe"), P()),
        out_specs=(P(None, "samp", "probe"), P(None, ("samp", "probe"))),
        check_vma=False,
    )
```

```python
import functools

import jax
import jax.numpy as jnp
from jax import lax
from jax.experimental import pallas as pl
from jax.experimental.pallas import tpu as pltpu
from jax.sharding import PartitionSpec as P

K = 32
ITERS = 128
GROUP = 16
PIECE = 2
BULK = (6, 9, 13, 17, 21)
RELAY = (0, 0, 0, 2, 5, 8, 12, 15)
EACH = 3
PACE = 3
LAGS = (1, 3, 5, 7, 9)
ORDER = (0, 1, 2, 3, 4, 5, 6, 7, 8, 9, 10, 11)
MESH = pl.DeviceIdType.MESH
F32 = jnp.float32
BF16 = jnp.bfloat16


def dot(a, b, dims=((1,), (0,))):
    return lax.dot_general(a, b, (dims, ((), ())), preferred_element_type=F32)


def copy_to(src, dst, send_sem, recv_sem, axis, peer):
    return pltpu.make_async_remote_copy(
        src_ref=src, dst_ref=dst, send_sem=send_sem, recv_sem=recv_sem,
        device_id={axis: peer}, device_id_type=MESH,
    )


def exchange_start(src_of, dst, send_sem, recv_sem, axis, peers, me):
    def body(step, carry):
        peer = lax.rem(me + step, peers)
        copy_to(src_of(peer), dst.at[me], send_sem, recv_sem, axis, peer).start()
        return carry
    lax.fori_loop(1, peers, body, 0)


def exchange_wait(dst, send_sem, recv_sem, axis, peers, me):
    rest = dst.at[pl.ds(0, peers - 1)]
    copy = copy_to(rest, rest, send_sem, recv_sem, axis, lax.rem(me + 1, peers))
    copy.wait_recv()
    copy.wait_send()


def pack(square):
    return jnp.concatenate([square[i * K // 4:(i + 1) * K // 4] for i in range(4)], axis=1)


def unpack(packed):
    return jnp.concatenate([packed[:, i * K:(i + 1) * K] for i in range(4)], axis=0)


def split3(value):
    high = value.astype(BF16)
    rest = value - high.astype(F32)
    mid = rest.astype(BF16)
    low = (rest - mid.astype(F32)).astype(BF16)
    return high, mid, low


def program_kernel(
    samps, probes_n, samples,
    methyl, atlas, ids, scores, out,
    pmsg, prcv, gcol, dmsg, drcv, cmsg, crcv, lmsg, lrcv, resid, smsg, srcv, lsplit,
    nmsg, nrcv, near, znat, raw, pown, pfar, pin, amsg, ain, fmsg, fin, bsum, ymsg, yin, final, xmsg, xin, sin, own4,
    psem, prsem, dsem, drsem, csem, crsem, lsem, lrsem, ssem, srsem,
    nsem, nrsem, msem, mrsem, rsem, rrsem, osem, orsem, zsem, zrsem, fsem, frsem, ysem, yrsem, xsem, xrsem, wsem, wrsem,
):
    me_p = lax.axis_index("probe")
    me_s = lax.axis_index("samp")
    blocks, share, cols = methyl.shape
    rows = blocks * share
    width = cols // samps
    phases = share // GROUP
    core = lax.rem(me_p, 2)
    z_at = lax.rem(me_p // 2, 4)
    y_at = me_p // 8
    sibling = me_p + 1 - 2 * core
    partner = me_p + 8 - 16 * y_at
    odd = lax.rem(me_s, 2)
    mate = me_s + 1 - 2 * odd
    cousin = lax.rem(me_s + samps - 1 + 2 * odd, samps)
    onward = lax.rem(me_s + samps + 2 - 4 * odd, samps)
    reach = cols // 2
    held = pl.ds(pl.multiple_of(odd * reach, reach), reach)
    given = pl.ds(pl.multiple_of((1 - odd) * reach, reach), reach)

    barrier = pltpu.get_barrier_semaphore()

    def greet(axis, peers, me):
        def body(step, carry):
            pl.semaphore_signal(
                barrier, inc=1, device_id={axis: lax.rem(me + step, peers)}, device_id_type=MESH
            )
            return carry
        lax.fori_loop(1, peers, body, 0)

    greet("samp", samps, me_s)
    greet("probe", probes_n, me_p)

    kinds = atlas.shape[0]
    select_t = (lax.broadcasted_iota(jnp.int32, (kinds, kinds), 0) == ids[...]).astype(F32)
    selector = select_t.T[:K].astype(BF16)
    panel = dot(selector, atlas[...]).astype(BF16)
    gram_part = dot(panel, panel, ((1,), (1,)))
    half = K // 2
    left = lax.broadcasted_iota(jnp.int32, (half, 128), 1) < share
    gram_rows = pack(gram_part)

    def project(step, carry):
        block = methyl[pl.ds(2 * step, 2)].reshape(2 * share, cols)
        part = dot(panel, block, ((1,), (1,)))
        top, low = part[:half], part[half:]
        pmsg[2 * step] = jnp.concatenate(
            [jnp.where(left, top, pltpu.roll(low, share, axis=1)), gram_rows], axis=0
        )
        pmsg[2 * step + 1] = jnp.concatenate(
            [jnp.where(left, pltpu.roll(top, share, axis=1), low), gram_rows], axis=0
        )
        return carry
    lax.fori_loop(0, probes_n // 2, project, 0)

    pl.semaphore_wait(barrier, probes_n - 1 + samps - 1)
    from_p = lambda peer: pmsg.at[peer]
    exchange_start(from_p, prcv, psem, prsem, "probe", probes_n, me_p)

    parts = blocks // PIECE
    pieces = phases * parts

    def place(piece):
        phase = piece // parts
        return phase, pl.ds((piece - phase * parts) * PIECE, PIECE)

    def bulk(piece):
        phase, at = place(piece)
        return copy_to(
            methyl.at[at, pl.ds(pl.multiple_of(phase * GROUP, GROUP), GROUP), given],
            raw.at[0, phase, at], msem, mrsem.at[piece], "samp", mate,
        )

    def relay(piece):
        phase, at = place(piece)
        return copy_to(
            raw.at[0, phase, at], raw.at[1, phase, at], rsem.at[piece], rrsem.at[piece], "samp", onward,
        )

    def bulk_start(first, past):
        def body(piece, carry):
            bulk(piece).start()
            return carry
        lax.fori_loop(first, past, body, 0)

    def relay_start(first, past):
        def body(piece, carry):
            bulk(piece).wait_recv()
            relay(piece).start()
            return carry
        lax.fori_loop(first, past, body, 0)

    prcv[me_p] = pmsg[me_p]
    exchange_wait(prcv, psem, prsem, "probe", probes_n, me_p)
    total = prcv[0]
    for peer in range(1, probes_n):
        total = total + prcv[peer]
    gram = unpack(total[half:])

    diag = lax.broadcasted_iota(jnp.int32, (K, K), 0) == lax.broadcasted_iota(jnp.int32, (K, K), 1)
    trace = jnp.sum(jnp.where(diag, gram, 0.0), axis=(0, 1), keepdims=True)
    rate = 1.0 / trace
    moving = jnp.where(diag, 1.0, 0.0) - gram * rate
    for k in range(K):
        gcol[k] = jnp.broadcast_to(moving[:, k:k + 1], (K, 128))
    goal = jnp.concatenate([total[:half], pltpu.roll(total[:half], share, axis=1)], axis=0) * rate

    def descend(step, state):
        sums = [goal, None]
        for k in range(K):
            term = gcol[k] * jnp.broadcast_to(state[k:k + 1, :], (K, 128))
            sums[k % 2] = term if sums[k % 2] is None else sums[k % 2] + term
        return jnp.maximum(sums[0] + sums[1], 0.0)
    bulk_start(0, BULK[0])
    state = jnp.full((K, 128), 1.0 / K, F32)
    for segment in range(4):
        state = lax.fori_loop(0, ITERS // 4, descend, state)
        if segment:
            relay_start(RELAY[segment - 1], RELAY[segment])
    weights = state[:, :share]
    scores[...] = weights * float(K)

    dmsg[...] = jnp.concatenate([weights[:half], weights[half:]], axis=1).astype(BF16)
    from_d = lambda peer: dmsg
    exchange_start(from_d, drcv, dsem, drsem, "probe", probes_n, me_p)
    drcv[me_p] = dmsg[...]
    exchange_wait(drcv, dsem, drsem, "probe", probes_n, me_p)
    columns = []
    for chip in range(probes_n // 2):
        one, two = drcv[2 * chip].astype(F32), drcv[2 * chip + 1].astype(F32)
        columns.append(jnp.concatenate([
            jnp.where(left, one, pltpu.roll(two, share, axis=1)),
            jnp.where(left, pltpu.roll(one, share, axis=1), two),
        ], axis=0))
    design_wide = jnp.concatenate(columns, axis=1)
    design = design_wide.astype(BF16)
    nmsg[...] = design

    def issue(slot):
        bulk_start(BULK[slot - 1], BULK[slot])
        relay_start(RELAY[slot + 2], RELAY[slot + 3])
    issue(1)

    wgram_part = dot(design, design, ((1,), (1,)))
    wrow = jnp.concatenate([pack(wgram_part), jnp.zeros((K // 4, width - 128), F32)], axis=1)

    def crossing(step, carry):
        at = pl.ds(pl.multiple_of(step * width, width), width)
        cmsg[step] = jnp.concatenate([dot(design, methyl[:, :, at].reshape(rows, width)), wrow], axis=0)
        return carry
    lax.fori_loop(0, samps, crossing, 0)
    from_c = lambda peer: cmsg.at[peer]
    exchange_start(from_c, crcv, csem, crsem, "samp", samps, me_s)
    crcv[me_s] = cmsg[me_s]
    own4[...] = jnp.concatenate([design_wide] * 4, axis=0).T.astype(BF16).reshape(blocks, share, 4 * K)
    exchange_wait(crcv, csem, crsem, "samp", samps, me_s)
    issue(2)
    both = crcv[0]
    for peer in range(1, samps):
        both = both + crcv[peer]

    matrix = jnp.concatenate([unpack(both[K:, :128]), jnp.zeros((K, 128 - K), F32)], axis=1)
    row_id = lax.broadcasted_iota(jnp.int32, (K, 128), 0)
    lane_id = lax.broadcasted_iota(jnp.int32, (K, 128), 1)
    matrix = matrix + jnp.where(row_id == lane_id, 0.0001 * samples, 0.0)
    right = both[:K]
    row_w = lax.broadcasted_iota(jnp.int32, (K, 1), 0)
    for k in range(K):
        column = matrix[:, k:k + 1]
        pivot = 1.0 / matrix[k:k + 1, k:k + 1]
        factor = jnp.where(row_w == k, 0.0, column * pivot)
        matrix_row = matrix[k:k + 1, :]
        right_row = right[k:k + 1, :]
        matrix = matrix - factor * matrix_row
        right = right - factor * right_row
    pivots = jnp.sum(jnp.where(row_id == lane_id, matrix, 0.0), axis=1, keepdims=True)
    lmsg[...] = right / pivots
    from_l = lambda peer: lmsg
    exchange_start(from_l, lrcv, lsem, lrsem, "samp", samps, me_s)
    lrcv[me_s] = lmsg[...]
    exchange_wait(lrcv, lsem, lrsem, "samp", samps, me_s)

    issue(3)
    part_blocks = 256 // share

    def residue(step, carry):
        high, mid, low = split3(lrcv[step])
        stacked = jnp.concatenate([high, mid, low, jnp.zeros_like(low)], axis=0)
        at = pl.ds(pl.multiple_of(step * width, width), width)
        lsplit[:, at] = stacked
        sums = jnp.zeros((1, width), F32)
        for b in range(0, blocks, part_blocks):
            res = methyl[b:b + part_blocks, :, at].reshape(256, width).astype(F32) - dot(
                own4[b:b + part_blocks].reshape(256, 4 * K), stacked
            )
            resid[b * share:b * share + 256, at] = res
            sums = sums + jnp.sum(res * res, axis=0, keepdims=True)
        smsg[:, at] = sums
        return carry
    lax.fori_loop(0, samps, residue, 0)
    from_s = lambda peer: smsg
    exchange_start(from_s, srcv, ssem, srsem, "samp", samps, me_s)
    srcv[me_s] = smsg[...]
    exchange_wait(srcv, ssem, srsem, "samp", samps, me_s)
    to_mate = copy_to(nmsg, nrcv.at[0], nsem.at[0], nrsem.at[0], "samp", mate)
    to_cousin = copy_to(nmsg, nrcv.at[1], nsem.at[1], nrsem.at[1], "samp", cousin)
    to_mate.start()
    to_cousin.start()
    issue(4)
    spread = srcv[0]
    for peer in range(1, samps):
        spread = spread + srcv[peer]
    smsg[...] = lax.rsqrt(spread * (1.0 / samples) + 1e-06)

    def normalize(step, carry):
        at = pl.ds(pl.multiple_of(step * width, width), width)
        for b in range(0, blocks, part_blocks):
            value = (resid[b * share:b * share + 256, at] * smsg[:, at]).astype(BF16)
            value = value.reshape(part_blocks, share, width)
            znat[b:b + part_blocks, :, at] = value
        return carry
    lax.fori_loop(0, samps, normalize, 0)

    def widen(which, copy):
        copy.wait_recv()
        others = nrcv[which].astype(F32)
        near[which] = jnp.concatenate([others] * 4, axis=0).T.astype(BF16).reshape(blocks, share, 4 * K)

    unit_rows = blocks * GROUP

    def to_sibling(unit):
        return copy_to(pfar.at[unit], pin.at[unit], osem, orsem.at[unit], "probe", sibling)

    def along_z(unit, way):
        z_to = lax.rem(z_at + 1 + 2 * way, 4)
        return copy_to(
            amsg.at[unit, way], ain.at[unit, way], zsem, zrsem.at[unit],
            "probe", y_at * 8 + z_to * 2 + core,
        )

    def far_z(unit, way):
        z_to = lax.rem(z_at + 1 + 2 * way, 4)
        return copy_to(
            fmsg.at[unit, way], fin.at[unit, way], fsem, frsem.at[unit],
            "probe", y_at * 8 + z_to * 2 + core,
        )

    def to_partner(unit):
        return copy_to(ymsg.at[unit], yin.at[unit], ysem, yrsem.at[unit], "probe", partner)

    pair = 2 * GROUP
    mine = me_p // 2

    def across(which, part, chip):
        return pltpu.make_async_remote_copy(
            src_ref=xmsg.at[which, pl.ds(part * pair, pair), pl.ds(pl.multiple_of(chip * 128, 128), 128)],
            dst_ref=xin.at[which, part, mine],
            send_sem=xsem, recv_sem=xrsem.at[which, part],
            device_id={"samp": (mate, cousin)[which], "probe": 2 * chip + core}, device_id_type=MESH,
        )

    def swap(which, part):
        return copy_to(xin.at[which, part], sin.at[which, part], wsem, wrsem.at[which, part], "probe", sibling)

    def arrived(src, dst, send_sem, recv_sem):
        return copy_to(src, dst, send_sem, recv_sem, "probe", sibling)

    def prepare(unit):
        which, phase = unit // phases - 1, unit % phases
        for piece in range(phase * parts, (phase + 1) * parts):
            if which:
                relay(piece).wait_recv()
            else:
                relay(piece).wait_send()
        group = near[which, :, pl.ds(pl.multiple_of(phase * GROUP, GROUP), GROUP), :].reshape(unit_rows, 4 * K)

        def body(step, carry):
            at = pl.ds(pl.multiple_of(step * width, width), width)
            there = pl.ds(pl.multiple_of(odd * reach + step * width, width), width)
            value = raw[which, phase, :, :, at].reshape(unit_rows, width).astype(F32)
            value = (value - dot(group, lsplit[:, there])) * smsg[:, there]
            raw[which, phase, :, :, at] = value.astype(BF16).reshape(blocks, GROUP, width)
            return carry
        lax.fori_loop(0, reach // width, body, 0)

    def put(unit, at, part):
        part = part.reshape(blocks // 2, 2, GROUP, 256)
        pown[unit, :, :, at] = jnp.where(core == 0, part[:, 0], part[:, 1])
        pfar[unit, :, :, at] = jnp.where(core == 0, part[:, 1], part[:, 0]).astype(BF16)

    def multiply(unit):
        which, phase = unit // phases - 1, unit % phases

        def body(step, carry):
            theirs = pl.ds(step * part_blocks, part_blocks)
            if unit < phases:
                group = znat[:, phase * GROUP:(phase + 1) * GROUP, :].reshape(unit_rows, cols)
                other = znat[theirs].reshape(256, cols)
            else:
                group = raw[which, phase].reshape(unit_rows, reach)
                other = znat[theirs, :, held].reshape(256, reach)
            put(unit, pl.ds(pl.multiple_of(step * 256, 256), 256), dot(group, other, ((1,), (1,))))
            return carry
        lax.fori_loop(0, rows // 256, body, 0)
        to_sibling(unit).start()

    def sum_cores(unit):
        to_sibling(unit).wait_recv()
        for block in range(blocks // 2):
            pown[unit, block] = pown[unit, block] + pin[unit, block].astype(F32)
        across_z = lax.rem(z_at + 2, 4)
        for way in range(2):
            fmsg[unit, way] = pown[unit, 4 * way + across_z].astype(BF16)
            far_z(unit, way).start()

    def sum_far(unit):
        arrived(fmsg.at[unit], fin.at[unit], fsem, frsem.at[unit]).wait_recv()
        for way in range(2):
            z_to = lax.rem(z_at + 1 + 2 * way, 4)
            amsg[unit, way, way] = (pown[unit, 4 * way + z_to] + fin[unit, way].astype(F32)).astype(BF16)
            amsg[unit, way, 1 - way] = pown[unit, 4 * (1 - way) + z_to].astype(BF16)
            along_z(unit, way).start()

    def sum_z(unit):
        arrived(amsg.at[unit], ain.at[unit], zsem, zrsem.at[unit]).wait_recv()
        for y in range(2):
            bsum[unit, y] = (
                pown[unit, 4 * y + z_at] + ain[unit, 0, y].astype(F32) + ain[unit, 1, y].astype(F32)
            )
        ymsg[unit] = bsum[unit, 1 - y_at].astype(BF16)
        to_partner(unit).start()

    def sum_y(unit):
        to_partner(unit).wait_recv()
        value = (bsum[unit, y_at] + yin[unit].astype(F32)) * (1.0 / (cols * probes_n))
        tile, phase = divmod(unit, phases)
        final[tile, phase * GROUP:(phase + 1) * GROUP] = value
        if tile:
            xmsg[tile - 1, phase * GROUP:(phase + 1) * GROUP] = value.astype(BF16)
        if tile and phase % 2:
            def send(step, carry):
                across(tile - 1, phase // 2, lax.rem(mine + step, blocks // 2)).start()
                return carry
            lax.fori_loop(0, blocks // 2, send, 0)

    def pass_on(unit):
        tile, phase = divmod(unit, phases)
        if tile and phase % 2:
            which, part = tile - 1, phase // 2
            arrived(xin.at[which, part], xin.at[which, part], xsem, xrsem.at[which, part]).wait_recv()
            swap(which, part).start()

    units = 3 * phases

    def assemble(which):
        for part in range(phases // 2):
            swap(which, part).wait_recv()
        for chip in range(blocks // 2):
            own, far = (
                jnp.concatenate([ref[which, part, chip] for part in range(phases // 2)], axis=0).astype(F32)
                for ref in (xin, sin)
            )
            rows_of_chip = jnp.concatenate(
                [jnp.where(core == 0, own, far), jnp.where(core == 0, far, own)], axis=0
            ).T
            at = slice(128 * chip, 128 * chip + 128)
            out[(2 - odd) if which == 0 else (1 + odd), :, at] = final[1 + which, :, at] + jnp.where(
                core == 0, rows_of_chip[:share], rows_of_chip[share:]
            )

    bulk_done, relay_done = BULK[4], RELAY[7]
    for turn in range(units + LAGS[4]):
        if turn == units + LAGS[4] - 2:
            out[0] = final[0]
            assemble(0)
        more = min(bulk_done + EACH, pieces)
        bulk_start(bulk_done, more)
        bulk_done = more
        if turn < units:
            unit = ORDER[turn]
            if unit in (phases, 2 * phases):
                widen(*((0, to_mate) if unit == phases else (1, to_cousin)))
            if phases <= unit < 2 * phases:
                more = max(relay_done, (unit - phases + 1) * parts)
                relay_start(relay_done, more)
                relay_done = more
            if unit >= phases:
                prepare(unit)
            multiply(unit)
        for lag, stage in zip(LAGS, (sum_cores, sum_far, sum_z, sum_y, pass_on)):
            if 0 <= turn - lag < units:
                stage(ORDER[turn - lag])
        more = min(max(relay_done, RELAY[7] + int(PACE * (turn + 1))), bulk_done)
        relay_start(relay_done, more)
        relay_done = more
    assemble(1)

    arrived(pfar, pin, osem, orsem.at[0]).wait_send()
    arrived(amsg, ain, zsem, zrsem.at[0]).wait_send()
    arrived(fmsg, fin, fsem, frsem.at[0]).wait_send()
    arrived(ymsg, yin, ysem, yrsem.at[0]).wait_send()
    arrived(xin, sin, xsem, wrsem.at[0, 0]).wait_send()
    arrived(xin, sin, wsem, wrsem.at[0, 0]).wait_send()
    arrived(raw.at[0], raw.at[1], msem, mrsem.at[0]).wait_send()
    to_mate.wait_send()
    to_cousin.wait_send()


def whole(mesh, methyl, atlas, panel_ids):
    samps, probes_n = mesh.shape["samp"], mesh.shape["probe"]
    rows, cols = methyl.shape
    share, width = rows // probes_n, cols // samps
    phases = share // GROUP
    units = 3 * phases
    pieces = phases * (probes_n // PIECE)
    per_core = probes_n // 2
    vmem = pl.BlockSpec(memory_space=pltpu.VMEM)
    dma = pltpu.SemaphoreType.DMA
    return pl.pallas_call(
        functools.partial(program_kernel, samps, probes_n, rows * samps),
        out_shape=(
            jax.ShapeDtypeStruct((K, share), F32),
            jax.ShapeDtypeStruct((3, share, rows), F32),
        ),
        in_specs=[vmem] * 3,
        out_specs=(vmem,) * 2,
        scratch_shapes=[
            pltpu.VMEM((probes_n, 3 * K // 4, 128), F32),
            pltpu.VMEM((probes_n, 3 * K // 4, 128), F32),
            pltpu.VMEM((K, K, 128), F32),
            pltpu.VMEM((K // 2, 128), BF16),
            pltpu.VMEM((probes_n, K // 2, 128), BF16),
            pltpu.VMEM((samps, 5 * K // 4, width), F32),
            pltpu.VMEM((samps, 5 * K // 4, width), F32),
            pltpu.VMEM((K, width), F32),
            pltpu.VMEM((samps, K, width), F32),
            pltpu.VMEM((rows, cols), F32),
            pltpu.VMEM((1, cols), F32),
            pltpu.VMEM((samps, 1, cols), F32),
            pltpu.VMEM((4 * K, cols), BF16),
            pltpu.VMEM((K, rows), BF16),
            pltpu.VMEM((2, K, rows), BF16),
            pltpu.VMEM((2, probes_n, share, 4 * K), BF16),
            pltpu.VMEM((probes_n, share, cols), BF16),
            pltpu.VMEM((2, phases, probes_n, GROUP, cols // 2), BF16),
            pltpu.VMEM((units, per_core, GROUP, rows), F32),
            pltpu.VMEM((units, per_core, GROUP, rows), BF16),
            pltpu.VMEM((units, per_core, GROUP, rows), BF16),
            pltpu.VMEM((units, 2, 2, GROUP, rows), BF16),
            pltpu.VMEM((units, 2, 2, GROUP, rows), BF16),
            pltpu.VMEM((units, 2, GROUP, rows), BF16),
            pltpu.VMEM((units, 2, GROUP, rows), BF16),
            pltpu.VMEM((units, 2, GROUP, rows), F32),
            pltpu.VMEM((units, GROUP, rows), BF16),
            pltpu.VMEM((units, GROUP, rows), BF16),
            pltpu.VMEM((3, share, rows), F32),
            pltpu.VMEM((2, share, rows), BF16),
            pltpu.VMEM((2, phases // 2, per_core, 2 * GROUP, 2 * share), BF16),
            pltpu.VMEM((2, phases // 2, per_core, 2 * GROUP, 2 * share), BF16),
            pltpu.VMEM((probes_n, share, 4 * K), BF16),
            dma, dma, dma, dma, dma, dma, dma, dma, dma, dma,
            dma((2,)), dma((2,)), dma, dma((pieces,)), dma((pieces,)), dma((pieces,)),
            dma, dma((units,)), dma, dma((units,)), dma, dma((units,)), dma, dma((units,)),
            dma, dma((2, phases // 2)), dma, dma((2, phases // 2)),
        ],
        compiler_params=pltpu.CompilerParams(
            collective_id=0, has_side_effects=True, vmem_limit_bytes=60 * 1024 * 1024
        ),
        name="whole",
    )(methyl.reshape(probes_n, share, cols), atlas, panel_ids.reshape(1, -1))


def solution(mesh):
    def body(methyl, atlas, panel_ids):
        scores, relmat = whole(mesh, methyl, atlas, panel_ids)
        return jnp.swapaxes(relmat, 1, 2), scores

    return jax.shard_map(
        body,
        mesh=mesh,
        in_specs=(P("samp", "probe"), P(None, "probe"), P()),
        out_specs=(P(None, "samp", "probe"), P(None, ("samp", "probe"))),
        check_vma=False,
    )
```

```python
import functools

import jax
import jax.numpy as jnp
from jax import lax
from jax.experimental import pallas as pl
from jax.experimental.pallas import tpu as pltpu
from jax.sharding import PartitionSpec as P

K = 32
ITERS = 128
GROUP = 16
PIECE = 2
BULK = (1, 6, 7, 10, 12, 15, 16, 19, 20, 23)
RELAY = (0, 0, 0, 3, 6, 9, 13, 16)
EACH = 3
PACE = 3
LAGS = (1, 3, 5, 7, 9)
LAGS_OWN = (1, 3, 5, 10, 11)
ORDER = (0, 1, 2, 3, 4, 5, 6, 7, 8, 9, 10, 11)
MESH = pl.DeviceIdType.MESH
F32 = jnp.float32
BF16 = jnp.bfloat16


def dot(a, b, dims=((1,), (0,))):
    return lax.dot_general(a, b, (dims, ((), ())), preferred_element_type=F32)


def copy_to(src, dst, send_sem, recv_sem, axis, peer):
    return pltpu.make_async_remote_copy(
        src_ref=src, dst_ref=dst, send_sem=send_sem, recv_sem=recv_sem,
        device_id={axis: peer}, device_id_type=MESH,
    )


def exchange_start(src_of, dst, send_sem, recv_sem, axis, peers, me):
    def body(step, carry):
        peer = lax.rem(me + step, peers)
        copy_to(src_of(peer), dst.at[me], send_sem, recv_sem, axis, peer).start()
        return carry
    lax.fori_loop(1, peers, body, 0)


def exchange_wait(dst, send_sem, recv_sem, axis, peers, me):
    rest = dst.at[pl.ds(0, peers - 1)]
    copy = copy_to(rest, rest, send_sem, recv_sem, axis, lax.rem(me + 1, peers))
    copy.wait_recv()
    copy.wait_send()


def pack(square):
    return jnp.concatenate([square[i * K // 4:(i + 1) * K // 4] for i in range(4)], axis=1)


def unpack(packed):
    return jnp.concatenate([packed[:, i * K:(i + 1) * K] for i in range(4)], axis=0)


def split3(value):
    high = value.astype(BF16)
    rest = value - high.astype(F32)
    mid = rest.astype(BF16)
    low = (rest - mid.astype(F32)).astype(BF16)
    return high, mid, low


def program_kernel(
    samps, probes_n, samples,
    methyl_in, atlas, ids, scores, out,
    methyl,
    pmsg, prcv, gcol, dmsg, drcv, cmsg, crcv, lmsg, lrcv, resid, smsg, srcv, lsplit,
    nmsg, nrcv, near, znat, raw, pown, pfar, pin, amsg, ain, fmsg, fin, bsum, ymsg, yin, final, xmsg, xin, sin, own4,
    psem, prsem, dsem, drsem, csem, crsem, lsem, lrsem, ssem, srsem,
    nsem, nrsem, msem, mrsem, rsem, rrsem, osem, orsem, zsem, zrsem, fsem, frsem, ysem, yrsem, xsem, xrsem, wsem, wrsem, insem,
):
    me_p = lax.axis_index("probe")
    me_s = lax.axis_index("samp")
    blocks, share, cols = methyl.shape
    rows = blocks * share
    width = cols // samps
    phases = share // GROUP
    core = lax.rem(me_p, 2)
    z_at = lax.rem(me_p // 2, 4)
    y_at = me_p // 8
    sibling = me_p + 1 - 2 * core
    partner = me_p + 8 - 16 * y_at
    odd = lax.rem(me_s, 2)
    mate = me_s + 1 - 2 * odd
    cousin = lax.rem(me_s + samps - 1 + 2 * odd, samps)
    onward = lax.rem(me_s + samps + 2 - 4 * odd, samps)
    reach = cols // 2
    held = pl.ds(pl.multiple_of(odd * reach, reach), reach)
    given = pl.ds(pl.multiple_of((1 - odd) * reach, reach), reach)

    barrier = pltpu.get_barrier_semaphore()

    def greet(axis, peers, me):
        def body(step, carry):
            pl.semaphore_signal(
                barrier, inc=1, device_id={axis: lax.rem(me + step, peers)}, device_id_type=MESH
            )
            return carry
        lax.fori_loop(1, peers, body, 0)

    greet("samp", samps, me_s)
    greet("probe", probes_n, me_p)

    quarter = blocks // 4

    def fetch(part):
        at = pl.ds(part * quarter, quarter)
        return pltpu.make_async_copy(methyl_in.at[at], methyl.at[at], insem.at[part])
    for part in range(4):
        fetch(part).start()

    kinds = atlas.shape[0]
    select_t = (lax.broadcasted_iota(jnp.int32, (kinds, kinds), 0) == ids[...]).astype(F32)
    selector = select_t.T[:K].astype(BF16)
    panel = dot(selector, atlas[...]).astype(BF16)
    gram_part = dot(panel, panel, ((1,), (1,)))
    half = K // 2
    left = lax.broadcasted_iota(jnp.int32, (half, 128), 1) < share
    gram_rows = pack(gram_part)

    def project(step, carry):
        block = methyl[pl.ds(2 * step, 2)].reshape(2 * share, cols)
        part = dot(panel, block, ((1,), (1,)))
        top, low = part[:half], part[half:]
        pmsg[2 * step] = jnp.concatenate(
            [jnp.where(left, top, pltpu.roll(low, share, axis=1)), gram_rows], axis=0
        )
        pmsg[2 * step + 1] = jnp.concatenate(
            [jnp.where(left, pltpu.roll(top, share, axis=1), low), gram_rows], axis=0
        )
        return carry
    for part in range(4):
        fetch(part).wait()
        lax.fori_loop(part * quarter // 2, (part + 1) * quarter // 2, project, 0)

    pl.semaphore_wait(barrier, probes_n - 1 + samps - 1)
    from_p = lambda peer: pmsg.at[peer]
    exchange_start(from_p, prcv, psem, prsem, "probe", probes_n, me_p)

    parts = blocks // PIECE
    pieces = phases * parts

    def place(piece):
        phase = piece // parts
        return phase, pl.ds((piece - phase * parts) * PIECE, PIECE)

    def bulk(piece):
        phase, at = place(piece)
        return copy_to(
            methyl.at[at, pl.ds(pl.multiple_of(phase * GROUP, GROUP), GROUP), given],
            raw.at[0, phase, at], msem, mrsem.at[piece], "samp", mate,
        )

    def relay(piece):
        phase, at = place(piece)
        return copy_to(
            raw.at[0, phase, at], raw.at[1, phase, at], rsem.at[piece], rrsem.at[piece], "samp", onward,
        )

    def bulk_start(first, past):
        def body(piece, carry):
            bulk(piece).start()
            return carry
        lax.fori_loop(first, past, body, 0)

    def relay_start(first, past):
        def body(piece, carry):
            bulk(piece).wait_recv()
            relay(piece).start()
            return carry
        lax.fori_loop(first, past, body, 0)

    bulk_start(0, BULK[0])
    prcv[me_p] = pmsg[me_p]
    exchange_wait(prcv, psem, prsem, "probe", probes_n, me_p)
    total = prcv[0]
    for peer in range(1, probes_n):
        total = total + prcv[peer]
    gram = unpack(total[half:])

    diag = lax.broadcasted_iota(jnp.int32, (K, K), 0) == lax.broadcasted_iota(jnp.int32, (K, K), 1)
    trace = jnp.sum(jnp.where(diag, gram, 0.0), axis=(0, 1), keepdims=True)
    rate = 1.0 / trace
    moving = jnp.where(diag, 1.0, 0.0) - gram * rate
    for k in range(K):
        gcol[k] = jnp.broadcast_to(moving[:, k:k + 1], (K, 128))
    goal = jnp.concatenate([total[:half], pltpu.roll(total[:half], share, axis=1)], axis=0) * rate

    def descend(step, state):
        sums = [goal, None]
        for k in range(K):
            term = gcol[k] * jnp.broadcast_to(state[k:k + 1, :], (K, 128))
            sums[k % 2] = term if sums[k % 2] is None else sums[k % 2] + term
        return jnp.maximum(sums[0] + sums[1], 0.0)
    bulk_start(BULK[0], BULK[1])
    state = jnp.full((K, 128), 1.0 / K, F32)
    for segment in range(4):
        state = lax.fori_loop(0, ITERS // 4, descend, state)
        if segment:
            relay_start(RELAY[segment - 1], RELAY[segment])
    weights = state[:, :share]
    scores[...] = weights * float(K)

    dmsg[...] = jnp.concatenate([weights[:half], weights[half:]], axis=1).astype(BF16)
    from_d = lambda peer: dmsg
    exchange_start(from_d, drcv, dsem, drsem, "probe", probes_n, me_p)
    bulk_start(BULK[1], BULK[2])
    drcv[me_p] = dmsg[...]
    exchange_wait(drcv, dsem, drsem, "probe", probes_n, me_p)
    columns = []
    for chip in range(probes_n // 2):
        one, two = drcv[2 * chip].astype(F32), drcv[2 * chip + 1].astype(F32)
        columns.append(jnp.concatenate([
            jnp.where(left, one, pltpu.roll(two, share, axis=1)),
            jnp.where(left, pltpu.roll(one, share, axis=1), two),
        ], axis=0))
    design_wide = jnp.concatenate(columns, axis=1)
    design = design_wide.astype(BF16)
    nmsg[...] = design

    def issue(slot):
        bulk_start(BULK[2 * slot], BULK[2 * slot + 1])
        relay_start(RELAY[slot + 2], RELAY[slot + 3])
    issue(1)

    wgram_part = dot(design, design, ((1,), (1,)))
    wrow = jnp.concatenate([pack(wgram_part), jnp.zeros((K // 4, width - 128), F32)], axis=1)

    def crossing(step, carry):
        at = pl.ds(pl.multiple_of(step * width, width), width)
        cmsg[step] = jnp.concatenate([dot(design, methyl[:, :, at].reshape(rows, width)), wrow], axis=0)
        return carry
    lax.fori_loop(0, samps, crossing, 0)
    from_c = lambda peer: cmsg.at[peer]
    exchange_start(from_c, crcv, csem, crsem, "samp", samps, me_s)
    bulk_start(BULK[3], BULK[4])
    crcv[me_s] = cmsg[me_s]
    own4[...] = jnp.concatenate([design_wide] * 4, axis=0).T.astype(BF16).reshape(blocks, share, 4 * K)
    exchange_wait(crcv, csem, crsem, "samp", samps, me_s)
    issue(2)
    both = crcv[0]
    for peer in range(1, samps):
        both = both + crcv[peer]

    matrix = jnp.concatenate([unpack(both[K:, :128]), jnp.zeros((K, 128 - K), F32)], axis=1)
    row_id = lax.broadcasted_iota(jnp.int32, (K, 128), 0)
    lane_id = lax.broadcasted_iota(jnp.int32, (K, 128), 1)
    matrix = matrix + jnp.where(row_id == lane_id, 0.0001 * samples, 0.0)
    right = both[:K]
    row_w = lax.broadcasted_iota(jnp.int32, (K, 1), 0)
    for k in range(K):
        column = matrix[:, k:k + 1]
        pivot = 1.0 / matrix[k:k + 1, k:k + 1]
        factor = jnp.where(row_w == k, 0.0, column * pivot)
        matrix_row = matrix[k:k + 1, :]
        right_row = right[k:k + 1, :]
        matrix = matrix - factor * matrix_row
        right = right - factor * right_row
    pivots = jnp.sum(jnp.where(row_id == lane_id, matrix, 0.0), axis=1, keepdims=True)
    lmsg[...] = right / pivots
    from_l = lambda peer: lmsg
    exchange_start(from_l, lrcv, lsem, lrsem, "samp", samps, me_s)
    bulk_start(BULK[5], BULK[6])
    lrcv[me_s] = lmsg[...]
    exchange_wait(lrcv, lsem, lrsem, "samp", samps, me_s)

    issue(3)
    part_blocks = 256 // share

    def residue(step, carry):
        high, mid, low = split3(lrcv[step])
        stacked = jnp.concatenate([high, mid, low, jnp.zeros_like(low)], axis=0)
        at = pl.ds(pl.multiple_of(step * width, width), width)
        lsplit[:, at] = stacked
        sums = jnp.zeros((1, width), F32)
        for b in range(0, blocks, part_blocks):
            res = methyl[b:b + part_blocks, :, at].reshape(256, width).astype(F32) - dot(
                own4[b:b + part_blocks].reshape(256, 4 * K), stacked
            )
            resid[b * share:b * share + 256, at] = res
            sums = sums + jnp.sum(res * res, axis=0, keepdims=True)
        smsg[:, at] = sums
        return carry
    lax.fori_loop(0, samps, residue, 0)
    from_s = lambda peer: smsg
    exchange_start(from_s, srcv, ssem, srsem, "samp", samps, me_s)
    bulk_start(BULK[7], BULK[8])
    srcv[me_s] = smsg[...]
    exchange_wait(srcv, ssem, srsem, "samp", samps, me_s)
    to_mate = copy_to(nmsg, nrcv.at[0], nsem.at[0], nrsem.at[0], "samp", mate)
    to_cousin = copy_to(nrcv.at[0], nrcv.at[1], nsem.at[1], nrsem.at[1], "samp", onward)
    to_mate.start()
    issue(4)
    spread = srcv[0]
    for peer in range(1, samps):
        spread = spread + srcv[peer]
    smsg[...] = lax.rsqrt(spread * (1.0 / samples) + 1e-06)

    def normalize(step, carry):
        at = pl.ds(pl.multiple_of(step * width, width), width)
        for b in range(0, blocks, part_blocks):
            value = (resid[b * share:b * share + 256, at] * smsg[:, at]).astype(BF16)
            value = value.reshape(part_blocks, share, width)
            znat[b:b + part_blocks, :, at] = value
        return carry
    lax.fori_loop(0, samps, normalize, 0)

    def widen(which, copy):
        copy.wait_recv()
        if which == 0:
            to_cousin.start()
        others = nrcv[which].astype(F32)
        near[which] = jnp.concatenate([others] * 4, axis=0).T.astype(BF16).reshape(blocks, share, 4 * K)

    unit_rows = blocks * GROUP

    def to_sibling(unit):
        return copy_to(pfar.at[unit], pin.at[unit], osem, orsem.at[unit], "probe", sibling)

    def along_z(unit, way):
        z_to = lax.rem(z_at + 1 + 2 * way, 4)
        return copy_to(
            amsg.at[unit, way], ain.at[unit, way], zsem, zrsem.at[unit],
            "probe", y_at * 8 + z_to * 2 + core,
        )

    def far_z(unit, way):
        z_to = lax.rem(z_at + 1 + 2 * way, 4)
        return copy_to(
            fmsg.at[unit, way], fin.at[unit, way], fsem, frsem.at[unit],
            "probe", y_at * 8 + z_to * 2 + core,
        )

    def to_partner(unit):
        return copy_to(ymsg.at[unit], yin.at[unit], ysem, yrsem.at[unit], "probe", partner)

    pair = 2 * GROUP
    mine = me_p // 2

    def across(which, part, chip):
        return pltpu.make_async_remote_copy(
            src_ref=xmsg.at[which, pl.ds(part * pair, pair), pl.ds(pl.multiple_of(chip * 128, 128), 128)],
            dst_ref=xin.at[which, part, mine],
            send_sem=xsem, recv_sem=xrsem.at[which, part],
            device_id={"samp": (mate, cousin)[which], "probe": 2 * chip + core}, device_id_type=MESH,
        )

    def swap(which, part):
        return copy_to(xin.at[which, part], sin.at[which, part], wsem, wrsem.at[which, part], "probe", sibling)

    def arrived(src, dst, send_sem, recv_sem):
        return copy_to(src, dst, send_sem, recv_sem, "probe", sibling)

    def prepare(unit):
        which, phase = unit // phases - 1, unit % phases
        for piece in range(phase * parts, (phase + 1) * parts):
            if which:
                relay(piece).wait_recv()
            else:
                relay(piece).wait_send()
        group = near[which, :, pl.ds(pl.multiple_of(phase * GROUP, GROUP), GROUP), :].reshape(unit_rows, 4 * K)

        def body(step, carry):
            at = pl.ds(pl.multiple_of(step * width, width), width)
            there = pl.ds(pl.multiple_of(odd * reach + step * width, width), width)
            value = raw[which, phase, :, :, at].reshape(unit_rows, width).astype(F32)
            value = (value - dot(group, lsplit[:, there])) * smsg[:, there]
            raw[which, phase, :, :, at] = value.astype(BF16).reshape(blocks, GROUP, width)
            return carry
        lax.fori_loop(0, reach // width, body, 0)

    def put(unit, at, part):
        part = part.reshape(blocks // 2, 2, GROUP, 256)
        pown[unit, :, :, at] = jnp.where(core == 0, part[:, 0], part[:, 1])
        pfar[unit, :, :, at] = jnp.where(core == 0, part[:, 1], part[:, 0]).astype(BF16)

    def multiply(unit):
        which, phase = unit // phases - 1, unit % phases

        def body(step, carry):
            theirs = pl.ds(step * part_blocks, part_blocks)
            if unit < phases:
                group = znat[:, phase * GROUP:(phase + 1) * GROUP, :].reshape(unit_rows, cols)
                other = znat[theirs].reshape(256, cols)
            else:
                group = raw[which, phase].reshape(unit_rows, reach)
                other = znat[theirs, :, held].reshape(256, reach)
            put(unit, pl.ds(pl.multiple_of(step * 256, 256), 256), dot(group, other, ((1,), (1,))))
            return carry
        lax.fori_loop(0, rows // 256, body, 0)
        to_sibling(unit).start()

    def sum_cores(unit):
        to_sibling(unit).wait_recv()
        for block in range(blocks // 2):
            pown[unit, block] = pown[unit, block] + pin[unit, block].astype(F32)
        across_z = lax.rem(z_at + 2, 4)
        for way in range(2):
            fmsg[unit, way] = pown[unit, 4 * way + across_z].astype(BF16)
            far_z(unit, way).start()

    def sum_far(unit):
        arrived(fmsg.at[unit], fin.at[unit], fsem, frsem.at[unit]).wait_recv()
        for way in range(2):
            z_to = lax.rem(z_at + 1 + 2 * way, 4)
            amsg[unit, way, way] = (pown[unit, 4 * way + z_to] + fin[unit, way].astype(F32)).astype(BF16)
            amsg[unit, way, 1 - way] = pown[unit, 4 * (1 - way) + z_to].astype(BF16)
            along_z(unit, way).start()

    def sum_z(unit):
        arrived(amsg.at[unit], ain.at[unit], zsem, zrsem.at[unit]).wait_recv()
        for y in range(2):
            bsum[unit, y] = (
                pown[unit, 4 * y + z_at] + ain[unit, 0, y].astype(F32) + ain[unit, 1, y].astype(F32)
            )
        ymsg[unit] = bsum[unit, 1 - y_at].astype(BF16)
        to_partner(unit).start()

    def sum_y(unit):
        to_partner(unit).wait_recv()
        value = (bsum[unit, y_at] + yin[unit].astype(F32)) * (1.0 / (cols * probes_n))
        tile, phase = divmod(unit, phases)
        final[tile, phase * GROUP:(phase + 1) * GROUP] = value
        if tile:
            xmsg[tile - 1, phase * GROUP:(phase + 1) * GROUP] = value.astype(BF16)
        if tile and phase % 2:
            def send(step, carry):
                across(tile - 1, phase // 2, lax.rem(mine + step, blocks // 2)).start()
                return carry
            lax.fori_loop(0, blocks // 2, send, 0)

    def pass_on(unit):
        tile, phase = divmod(unit, phases)
        if tile and phase % 2:
            which, part = tile - 1, phase // 2
            arrived(xin.at[which, part], xin.at[which, part], xsem, xrsem.at[which, part]).wait_recv()
            swap(which, part).start()

    units = 3 * phases

    def assemble(which):
        for part in range(phases // 2):
            swap(which, part).wait_recv()
        for chip in range(blocks // 2):
            own, far = (
                jnp.concatenate([ref[which, part, chip] for part in range(phases // 2)], axis=0).astype(F32)
                for ref in (xin, sin)
            )
            rows_of_chip = jnp.concatenate(
                [jnp.where(core == 0, own, far), jnp.where(core == 0, far, own)], axis=0
            ).T
            at = slice(128 * chip, 128 * chip + 128)
            out[(2 - odd) if which == 0 else (1 + odd), :, at] = final[1 + which, :, at] + jnp.where(
                core == 0, rows_of_chip[:share], rows_of_chip[share:]
            )

    bulk_done, relay_done = BULK[9], RELAY[7]
    for turn in range(units + LAGS[4]):
        if turn == units + LAGS[4] - 2:
            out[0] = final[0]
            assemble(0)
        more = min(bulk_done + EACH, pieces)
        bulk_start(bulk_done, more)
        bulk_done = more
        if turn < units:
            unit = ORDER[turn]
            if unit in (phases, 2 * phases):
                widen(*((0, to_mate) if unit == phases else (1, to_cousin)))
            if phases <= unit < 2 * phases:
                more = max(relay_done, (unit - phases + 1) * parts)
                relay_start(relay_done, more)
                relay_done = more
            if unit >= phases:
                prepare(unit)
            multiply(unit)
        for number, stage in enumerate((sum_cores, sum_far, sum_z, sum_y, pass_on)):
            for spot, unit in enumerate(ORDER):
                if turn - spot == (LAGS_OWN if unit < phases else LAGS)[number]:
                    stage(unit)
        more = min(max(relay_done, RELAY[7] + int(PACE * (turn + 1))), bulk_done)
        relay_start(relay_done, more)
        relay_done = more
    assemble(1)

    arrived(pfar, pin, osem, orsem.at[0]).wait_send()
    arrived(amsg, ain, zsem, zrsem.at[0]).wait_send()
    arrived(fmsg, fin, fsem, frsem.at[0]).wait_send()
    arrived(ymsg, yin, ysem, yrsem.at[0]).wait_send()
    arrived(xin, sin, xsem, wrsem.at[0, 0]).wait_send()
    arrived(xin, sin, wsem, wrsem.at[0, 0]).wait_send()
    arrived(raw.at[0], raw.at[1], msem, mrsem.at[0]).wait_send()
    to_mate.wait_send()
    to_cousin.wait_send()


def whole(mesh, methyl, atlas, panel_ids):
    samps, probes_n = mesh.shape["samp"], mesh.shape["probe"]
    rows, cols = methyl.shape
    share, width = rows // probes_n, cols // samps
    phases = share // GROUP
    units = 3 * phases
    pieces = phases * (probes_n // PIECE)
    per_core = probes_n // 2
    vmem = pl.BlockSpec(memory_space=pltpu.VMEM)
    dma = pltpu.SemaphoreType.DMA
    return pl.pallas_call(
        functools.partial(program_kernel, samps, probes_n, rows * samps),
        out_shape=(
            jax.ShapeDtypeStruct((K, share), F32),
            jax.ShapeDtypeStruct((3, share, rows), F32),
        ),
        in_specs=[pl.BlockSpec(memory_space=pl.ANY), vmem, vmem],
        out_specs=(vmem,) * 2,
        scratch_shapes=[
            pltpu.VMEM((probes_n, share, cols), BF16),
            pltpu.VMEM((probes_n, 3 * K // 4, 128), F32),
            pltpu.VMEM((probes_n, 3 * K // 4, 128), F32),
            pltpu.VMEM((K, K, 128), F32),
            pltpu.VMEM((K // 2, 128), BF16),
            pltpu.VMEM((probes_n, K // 2, 128), BF16),
            pltpu.VMEM((samps, 5 * K // 4, width), F32),
            pltpu.VMEM((samps, 5 * K // 4, width), F32),
            pltpu.VMEM((K, width), F32),
            pltpu.VMEM((samps, K, width), F32),
            pltpu.VMEM((rows, cols), F32),
            pltpu.VMEM((1, cols), F32),
            pltpu.VMEM((samps, 1, cols), F32),
            pltpu.VMEM((4 * K, cols), BF16),
            pltpu.VMEM((K, rows), BF16),
            pltpu.VMEM((2, K, rows), BF16),
            pltpu.VMEM((2, probes_n, share, 4 * K), BF16),
            pltpu.VMEM((probes_n, share, cols), BF16),
            pltpu.VMEM((2, phases, probes_n, GROUP, cols // 2), BF16),
            pltpu.VMEM((units, per_core, GROUP, rows), F32),
            pltpu.VMEM((units, per_core, GROUP, rows), BF16),
            pltpu.VMEM((units, per_core, GROUP, rows), BF16),
            pltpu.VMEM((units, 2, 2, GROUP, rows), BF16),
            pltpu.VMEM((units, 2, 2, GROUP, rows), BF16),
            pltpu.VMEM((units, 2, GROUP, rows), BF16),
            pltpu.VMEM((units, 2, GROUP, rows), BF16),
            pltpu.VMEM((units, 2, GROUP, rows), F32),
            pltpu.VMEM((units, GROUP, rows), BF16),
            pltpu.VMEM((units, GROUP, rows), BF16),
            pltpu.VMEM((3, share, rows), F32),
            pltpu.VMEM((2, share, rows), BF16),
            pltpu.VMEM((2, phases // 2, per_core, 2 * GROUP, 2 * share), BF16),
            pltpu.VMEM((2, phases // 2, per_core, 2 * GROUP, 2 * share), BF16),
            pltpu.VMEM((probes_n, share, 4 * K), BF16),
            dma, dma, dma, dma, dma, dma, dma, dma, dma, dma,
            dma((2,)), dma((2,)), dma, dma((pieces,)), dma((pieces,)), dma((pieces,)),
            dma, dma((units,)), dma, dma((units,)), dma, dma((units,)), dma, dma((units,)),
            dma, dma((2, phases // 2)), dma, dma((2, phases // 2)), dma((4,)),
        ],
        compiler_params=pltpu.CompilerParams(
            collective_id=0, has_side_effects=True, vmem_limit_bytes=60 * 1024 * 1024
        ),
        name="whole",
    )(methyl.reshape(probes_n, share, cols), atlas, panel_ids.reshape(1, -1))


def solution(mesh):
    def body(methyl, atlas, panel_ids):
        scores, relmat = whole(mesh, methyl, atlas, panel_ids)
        return jnp.swapaxes(relmat, 1, 2), scores

    return jax.shard_map(
        body,
        mesh=mesh,
        in_specs=(P("samp", "probe"), P(None, "probe"), P()),
        out_specs=(P(None, "samp", "probe"), P(None, ("samp", "probe"))),
        check_vma=False,
    )
```

```python
import functools

import jax
import jax.numpy as jnp
from jax import lax
from jax.experimental import pallas as pl
from jax.experimental.pallas import tpu as pltpu
from jax.sharding import PartitionSpec as P

K = 32
ITERS = 128
GROUP = 16
PIECE = 2
BULK = (1, 6, 7, 10, 12, 15, 17, 20, 22, 25)
RELAY = (0, 0, 0, 3, 6, 9, 13, 16)
EACH = 3
PACE = 3
LAGS = (1, 3, 5, 7, 9)
LAGS_OWN = (1, 3, 5, 10, 11)
ORDER = (0, 1, 2, 3, 4, 5, 6, 7, 8, 9, 10, 11)
MESH = pl.DeviceIdType.MESH
F32 = jnp.float32
BF16 = jnp.bfloat16


def dot(a, b, dims=((1,), (0,))):
    return lax.dot_general(a, b, (dims, ((), ())), preferred_element_type=F32)


def copy_to(src, dst, send_sem, recv_sem, axis, peer):
    return pltpu.make_async_remote_copy(
        src_ref=src, dst_ref=dst, send_sem=send_sem, recv_sem=recv_sem,
        device_id={axis: peer}, device_id_type=MESH,
    )


def exchange_start(src_of, dst, send_sem, recv_sem, axis, peers, me):
    def body(step, carry):
        peer = lax.rem(me + step, peers)
        copy_to(src_of(peer), dst.at[me], send_sem, recv_sem, axis, peer).start()
        return carry
    lax.fori_loop(1, peers, body, 0)


def exchange_wait(dst, send_sem, recv_sem, axis, peers, me):
    rest = dst.at[pl.ds(0, peers - 1)]
    copy = copy_to(rest, rest, send_sem, recv_sem, axis, lax.rem(me + 1, peers))
    copy.wait_recv()
    copy.wait_send()


def pack(square):
    return jnp.concatenate([square[i * K // 4:(i + 1) * K // 4] for i in range(4)], axis=1)


def unpack(packed):
    return jnp.concatenate([packed[:, i * K:(i + 1) * K] for i in range(4)], axis=0)


def split3(value):
    high = value.astype(BF16)
    rest = value - high.astype(F32)
    mid = rest.astype(BF16)
    low = (rest - mid.astype(F32)).astype(BF16)
    return high, mid, low


def program_kernel(
    samps, probes_n, samples,
    methyl_in, atlas, ids, scores, out,
    methyl,
    pmsg, prcv, gcol, dmsg, drcv, cmsg, crcv, lmsg, lrcv, resid, smsg, srcv, lsplit,
    nmsg, nrcv, near, znat, raw, pown, pfar, pin, amsg, ain, fmsg, fin, bsum, ymsg, yin, final, xmsg, xin, sin, own4,
    psem, prsem, dsem, drsem, csem, crsem, lsem, lrsem, ssem, srsem,
    nsem, nrsem, msem, mrsem, rsem, rrsem, osem, orsem, zsem, zrsem, fsem, frsem, ysem, yrsem, xsem, xrsem, wsem, wrsem, insem,
):
    me_p = lax.axis_index("probe")
    me_s = lax.axis_index("samp")
    blocks, share, cols = methyl.shape
    rows = blocks * share
    width = cols // samps
    phases = share // GROUP
    core = lax.rem(me_p, 2)
    z_at = lax.rem(me_p // 2, 4)
    y_at = me_p // 8
    sibling = me_p + 1 - 2 * core
    partner = me_p + 8 - 16 * y_at
    odd = lax.rem(me_s, 2)
    mate = me_s + 1 - 2 * odd
    cousin = lax.rem(me_s + samps - 1 + 2 * odd, samps)
    onward = lax.rem(me_s + samps + 2 - 4 * odd, samps)
    reach = cols // 2
    held = pl.ds(pl.multiple_of(odd * reach, reach), reach)
    given = pl.ds(pl.multiple_of((1 - odd) * reach, reach), reach)

    barrier = pltpu.get_barrier_semaphore()

    def greet(axis, peers, me):
        def body(step, carry):
            pl.semaphore_signal(
                barrier, inc=1, device_id={axis: lax.rem(me + step, peers)}, device_id_type=MESH
            )
            return carry
        lax.fori_loop(1, peers, body, 0)

    greet("samp", samps, me_s)
    greet("probe", probes_n, me_p)

    quarter = blocks // 4

    def fetch(part):
        at = pl.ds(part * quarter, quarter)
        return pltpu.make_async_copy(methyl_in.at[at], methyl.at[at], insem.at[part])
    for part in range(4):
        fetch(part).start()

    kinds = atlas.shape[0]
    select_t = (lax.broadcasted_iota(jnp.int32, (kinds, kinds), 0) == ids[...]).astype(F32)
    selector = select_t.T[:K].astype(BF16)
    panel = dot(selector, atlas[...]).astype(BF16)
    gram_part = dot(panel, panel, ((1,), (1,)))
    half = K // 2
    left = lax.broadcasted_iota(jnp.int32, (half, 128), 1) < share
    gram_rows = pack(gram_part)

    def project(step, carry):
        block = methyl[pl.ds(2 * step, 2)].reshape(2 * share, cols)
        part = dot(panel, block, ((1,), (1,)))
        top, low = part[:half], part[half:]
        pmsg[2 * step] = jnp.concatenate(
            [jnp.where(left, top, pltpu.roll(low, share, axis=1)), gram_rows], axis=0
        )
        pmsg[2 * step + 1] = jnp.concatenate(
            [jnp.where(left, pltpu.roll(top, share, axis=1), low), gram_rows], axis=0
        )
        return carry
    for part in range(4):
        fetch(part).wait()
        lax.fori_loop(part * quarter // 2, (part + 1) * quarter // 2, project, 0)

    pl.semaphore_wait(barrier, probes_n - 1 + samps - 1)
    from_p = lambda peer: pmsg.at[peer]
    exchange_start(from_p, prcv, psem, prsem, "probe", probes_n, me_p)

    parts = blocks // PIECE
    pieces = phases * parts

    def place(piece):
        phase = piece // parts
        return phase, pl.ds((piece - phase * parts) * PIECE, PIECE)

    def bulk(piece):
        phase, at = place(piece)
        return copy_to(
            methyl.at[at, pl.ds(pl.multiple_of(phase * GROUP, GROUP), GROUP), given],
            raw.at[0, phase, at], msem, mrsem.at[piece], "samp", mate,
        )

    def relay(piece):
        phase, at = place(piece)
        return copy_to(
            raw.at[0, phase, at], raw.at[1, phase, at], rsem.at[piece], rrsem.at[piece], "samp", onward,
        )

    def bulk_start(first, past):
        def body(piece, carry):
            bulk(piece).start()
            return carry
        lax.fori_loop(first, past, body, 0)

    def relay_start(first, past):
        def body(piece, carry):
            bulk(piece).wait_recv()
            relay(piece).start()
            return carry
        lax.fori_loop(first, past, body, 0)

    bulk_start(0, BULK[0])
    prcv[me_p] = pmsg[me_p]
    exchange_wait(prcv, psem, prsem, "probe", probes_n, me_p)
    total = prcv[0]
    for peer in range(1, probes_n):
        total = total + prcv[peer]
    gram = unpack(total[half:])

    diag = lax.broadcasted_iota(jnp.int32, (K, K), 0) == lax.broadcasted_iota(jnp.int32, (K, K), 1)
    trace = jnp.sum(jnp.where(diag, gram, 0.0), axis=(0, 1), keepdims=True)
    rate = 1.0 / trace
    moving = jnp.where(diag, 1.0, 0.0) - gram * rate
    for k in range(K):
        gcol[k] = jnp.broadcast_to(moving[:, k:k + 1], (K, 128))
    goal = jnp.concatenate([total[:half], pltpu.roll(total[:half], share, axis=1)], axis=0) * rate

    def descend(step, state):
        sums = [goal, None]
        for k in range(K):
            term = gcol[k] * jnp.broadcast_to(state[k:k + 1, :], (K, 128))
            sums[k % 2] = term if sums[k % 2] is None else sums[k % 2] + term
        return jnp.maximum(sums[0] + sums[1], 0.0)
    bulk_start(BULK[0], BULK[1])
    state = jnp.full((K, 128), 1.0 / K, F32)
    for segment in range(4):
        state = lax.fori_loop(0, ITERS // 4, descend, state)
        if segment:
            relay_start(RELAY[segment - 1], RELAY[segment])
    weights = state[:, :share]
    scores[...] = weights * float(K)

    dmsg[...] = jnp.concatenate([weights[:half], weights[half:]], axis=1).astype(BF16)
    from_d = lambda peer: dmsg
    exchange_start(from_d, drcv, dsem, drsem, "probe", probes_n, me_p)
    bulk_start(BULK[1], BULK[2])
    drcv[me_p] = dmsg[...]
    exchange_wait(drcv, dsem, drsem, "probe", probes_n, me_p)
    columns = []
    for chip in range(probes_n // 2):
        one, two = drcv[2 * chip].astype(F32), drcv[2 * chip + 1].astype(F32)
        columns.append(jnp.concatenate([
            jnp.where(left, one, pltpu.roll(two, share, axis=1)),
            jnp.where(left, pltpu.roll(one, share, axis=1), two),
        ], axis=0))
    design_wide = jnp.concatenate(columns, axis=1)
    design = design_wide.astype(BF16)
    nmsg[...] = design

    def issue(slot):
        bulk_start(BULK[2 * slot], BULK[2 * slot + 1])
        relay_start(RELAY[slot + 2], RELAY[slot + 3])
    issue(1)

    wgram_part = dot(design, design, ((1,), (1,)))
    wrow = jnp.concatenate([pack(wgram_part), jnp.zeros((K // 4, width - 128), F32)], axis=1)

    def crossing(step, carry):
        at = pl.ds(pl.multiple_of(step * width, width), width)
        cmsg[step] = jnp.concatenate([dot(design, methyl[:, :, at].reshape(rows, width)), wrow], axis=0)
        return carry
    lax.fori_loop(0, samps, crossing, 0)
    from_c = lambda peer: cmsg.at[peer]
    exchange_start(from_c, crcv, csem, crsem, "samp", samps, me_s)
    bulk_start(BULK[3], BULK[4])
    crcv[me_s] = cmsg[me_s]
    own4[...] = jnp.concatenate([design_wide] * 4, axis=0).T.astype(BF16).reshape(blocks, share, 4 * K)
    exchange_wait(crcv, csem, crsem, "samp", samps, me_s)
    issue(2)
    both = crcv[0]
    for peer in range(1, samps):
        both = both + crcv[peer]

    matrix = jnp.concatenate([unpack(both[K:, :128]), jnp.zeros((K, 128 - K), F32)], axis=1)
    row_id = lax.broadcasted_iota(jnp.int32, (K, 128), 0)
    lane_id = lax.broadcasted_iota(jnp.int32, (K, 128), 1)
    matrix = matrix + jnp.where(row_id == lane_id, 0.0001 * samples, 0.0)
    right = both[:K]
    row_w = lax.broadcasted_iota(jnp.int32, (K, 1), 0)
    for k in range(K):
        column = matrix[:, k:k + 1]
        pivot = 1.0 / matrix[k:k + 1, k:k + 1]
        factor = jnp.where(row_w == k, 0.0, column * pivot)
        matrix_row = matrix[k:k + 1, :]
        right_row = right[k:k + 1, :]
        matrix = matrix - factor * matrix_row
        right = right - factor * right_row
    pivots = jnp.sum(jnp.where(row_id == lane_id, matrix, 0.0), axis=1, keepdims=True)
    lmsg[...] = right / pivots
    from_l = lambda peer: lmsg
    exchange_start(from_l, lrcv, lsem, lrsem, "samp", samps, me_s)
    bulk_start(BULK[5], BULK[6])
    lrcv[me_s] = lmsg[...]
    exchange_wait(lrcv, lsem, lrsem, "samp", samps, me_s)

    issue(3)
    part_blocks = 256 // share

    def residue(step, carry):
        high, mid, low = split3(lrcv[step])
        stacked = jnp.concatenate([high, mid, low, jnp.zeros_like(low)], axis=0)
        at = pl.ds(pl.multiple_of(step * width, width), width)
        lsplit[:, at] = stacked
        sums = jnp.zeros((1, width), F32)
        for b in range(0, blocks, part_blocks):
            res = methyl[b:b + part_blocks, :, at].reshape(256, width).astype(F32) - dot(
                own4[b:b + part_blocks].reshape(256, 4 * K), stacked
            )
            resid[b * share:b * share + 256, at] = res
            sums = sums + jnp.sum(res * res, axis=0, keepdims=True)
        smsg[:, at] = sums
        return carry
    lax.fori_loop(0, samps, residue, 0)
    from_s = lambda peer: smsg
    exchange_start(from_s, srcv, ssem, srsem, "samp", samps, me_s)
    bulk_start(BULK[7], BULK[8])
    srcv[me_s] = smsg[...]
    exchange_wait(srcv, ssem, srsem, "samp", samps, me_s)
    to_mate = copy_to(nmsg, nrcv.at[0], nsem.at[0], nrsem.at[0], "samp", mate)
    to_cousin = copy_to(nrcv.at[0], nrcv.at[1], nsem.at[1], nrsem.at[1], "samp", onward)
    to_mate.start()
    issue(4)
    spread = srcv[0]
    for peer in range(1, samps):
        spread = spread + srcv[peer]
    smsg[...] = lax.rsqrt(spread * (1.0 / samples) + 1e-06)

    def normalize(step, carry):
        at = pl.ds(pl.multiple_of(step * width, width), width)
        for b in range(0, blocks, part_blocks):
            value = (resid[b * share:b * share + 256, at] * smsg[:, at]).astype(BF16)
            value = value.reshape(part_blocks, share, width)
            znat[b:b + part_blocks, :, at] = value
        return carry
    lax.fori_loop(0, samps, normalize, 0)

    def widen(which, copy):
        copy.wait_recv()
        if which == 0:
            to_cousin.start()
        others = nrcv[which].astype(F32)
        near[which] = jnp.concatenate([others] * 4, axis=0).T.astype(BF16).reshape(blocks, share, 4 * K)

    unit_rows = blocks * GROUP

    def to_sibling(unit):
        return copy_to(pfar.at[unit], pin.at[unit], osem, orsem.at[unit], "probe", sibling)

    def along_z(unit, way):
        z_to = lax.rem(z_at + 1 + 2 * way, 4)
        return copy_to(
            amsg.at[unit, way], ain.at[unit, way], zsem, zrsem.at[unit],
            "probe", y_at * 8 + z_to * 2 + core,
        )

    def far_z(unit, way):
        z_to = lax.rem(z_at + 1 + 2 * way, 4)
        return copy_to(
            fmsg.at[unit, way], fin.at[unit, way], fsem, frsem.at[unit],
            "probe", y_at * 8 + z_to * 2 + core,
        )

    def to_partner(unit):
        return copy_to(ymsg.at[unit], yin.at[unit], ysem, yrsem.at[unit], "probe", partner)

    pair = 2 * GROUP
    mine = me_p // 2

    def across(which, part, chip):
        return pltpu.make_async_remote_copy(
            src_ref=xmsg.at[which, pl.ds(part * pair, pair), pl.ds(pl.multiple_of(chip * 128, 128), 128)],
            dst_ref=xin.at[which, part, mine],
            send_sem=xsem, recv_sem=xrsem.at[which, part],
            device_id={"samp": (mate, cousin)[which], "probe": 2 * chip + core}, device_id_type=MESH,
        )

    def swap(which, part):
        return copy_to(xin.at[which, part], sin.at[which, part], wsem, wrsem.at[which, part], "probe", sibling)

    def arrived(src, dst, send_sem, recv_sem):
        return copy_to(src, dst, send_sem, recv_sem, "probe", sibling)

    def prepare(unit):
        which, phase = unit // phases - 1, unit % phases
        for piece in range(phase * parts, (phase + 1) * parts):
            if which:
                relay(piece).wait_recv()
            else:
                relay(piece).wait_send()
        group = near[which, :, pl.ds(pl.multiple_of(phase * GROUP, GROUP), GROUP), :].reshape(unit_rows, 4 * K)

        def body(step, carry):
            at = pl.ds(pl.multiple_of(step * width, width), width)
            there = pl.ds(pl.multiple_of(odd * reach + step * width, width), width)
            value = raw[which, phase, :, :, at].reshape(unit_rows, width).astype(F32)
            value = (value - dot(group, lsplit[:, there])) * smsg[:, there]
            raw[which, phase, :, :, at] = value.astype(BF16).reshape(blocks, GROUP, width)
            return carry
        lax.fori_loop(0, reach // width, body, 0)

    def put(unit, at, part):
        part = part.reshape(blocks // 2, 2, GROUP, 256)
        pown[unit, :, :, at] = jnp.where(core == 0, part[:, 0], part[:, 1])
        pfar[unit, :, :, at] = jnp.where(core == 0, part[:, 1], part[:, 0]).astype(BF16)

    def multiply(unit):
        which, phase = unit // phases - 1, unit % phases

        def body(step, carry):
            theirs = pl.ds(step * part_blocks, part_blocks)
            if unit < phases:
                group = znat[:, phase * GROUP:(phase + 1) * GROUP, :].reshape(unit_rows, cols)
                other = znat[theirs].reshape(256, cols)
            else:
                group = raw[which, phase].reshape(unit_rows, reach)
                other = znat[theirs, :, held].reshape(256, reach)
            put(unit, pl.ds(pl.multiple_of(step * 256, 256), 256), dot(group, other, ((1,), (1,))))
            return carry
        lax.fori_loop(0, rows // 256, body, 0)
        to_sibling(unit).start()

    def sum_cores(unit):
        to_sibling(unit).wait_recv()
        for block in range(blocks // 2):
            pown[unit, block] = pown[unit, block] + pin[unit, block].astype(F32)
        across_z = lax.rem(z_at + 2, 4)
        for way in range(2):
            fmsg[unit, way] = pown[unit, 4 * way + across_z].astype(BF16)
            far_z(unit, way).start()

    def sum_far(unit):
        arrived(fmsg.at[unit], fin.at[unit], fsem, frsem.at[unit]).wait_recv()
        for way in range(2):
            z_to = lax.rem(z_at + 1 + 2 * way, 4)
            amsg[unit, way, way] = (pown[unit, 4 * way + z_to] + fin[unit, way].astype(F32)).astype(BF16)
            amsg[unit, way, 1 - way] = pown[unit, 4 * (1 - way) + z_to].astype(BF16)
            along_z(unit, way).start()

    def sum_z(unit):
        arrived(amsg.at[unit], ain.at[unit], zsem, zrsem.at[unit]).wait_recv()
        for y in range(2):
            bsum[unit, y] = (
                pown[unit, 4 * y + z_at] + ain[unit, 0, y].astype(F32) + ain[unit, 1, y].astype(F32)
            )
        ymsg[unit] = bsum[unit, 1 - y_at].astype(BF16)
        to_partner(unit).start()

    def sum_y(unit):
        to_partner(unit).wait_recv()
        value = (bsum[unit, y_at] + yin[unit].astype(F32)) * (1.0 / (cols * probes_n))
        tile, phase = divmod(unit, phases)
        final[tile, phase * GROUP:(phase + 1) * GROUP] = value
        if tile:
            xmsg[tile - 1, phase * GROUP:(phase + 1) * GROUP] = value.astype(BF16)
        if tile and phase % 2:
            def send(step, carry):
                across(tile - 1, phase // 2, lax.rem(mine + step, blocks // 2)).start()
                return carry
            lax.fori_loop(0, blocks // 2, send, 0)

    def pass_on(unit):
        tile, phase = divmod(unit, phases)
        if tile and phase % 2:
            which, part = tile - 1, phase // 2
            arrived(xin.at[which, part], xin.at[which, part], xsem, xrsem.at[which, part]).wait_recv()
            swap(which, part).start()

    units = 3 * phases

    def assemble(which):
        for part in range(phases // 2):
            swap(which, part).wait_recv()
        for chip in range(blocks // 2):
            own, far = (
                jnp.concatenate([ref[which, part, chip] for part in range(phases // 2)], axis=0).astype(F32)
                for ref in (xin, sin)
            )
            rows_of_chip = jnp.concatenate(
                [jnp.where(core == 0, own, far), jnp.where(core == 0, far, own)], axis=0
            ).T
            at = slice(128 * chip, 128 * chip + 128)
            out[(2 - odd) if which == 0 else (1 + odd), :, at] = final[1 + which, :, at] + jnp.where(
                core == 0, rows_of_chip[:share], rows_of_chip[share:]
            )

    bulk_done, relay_done = BULK[9], RELAY[7]
    for turn in range(units + LAGS[4]):
        if turn == units + LAGS[4] - 2:
            out[0] = final[0]
            assemble(0)
        more = min(bulk_done + EACH, pieces)
        bulk_start(bulk_done, more)
        bulk_done = more
        if turn < units:
            unit = ORDER[turn]
            if unit in (phases, 2 * phases):
                widen(*((0, to_mate) if unit == phases else (1, to_cousin)))
            if phases <= unit < 2 * phases:
                more = max(relay_done, (unit - phases + 1) * parts)
                relay_start(relay_done, more)
                relay_done = more
            if unit >= phases:
                prepare(unit)
            multiply(unit)
        for number, stage in enumerate((sum_cores, sum_far, sum_z, sum_y, pass_on)):
            for spot, unit in enumerate(ORDER):
                if turn - spot == (LAGS_OWN if unit < phases else LAGS)[number]:
                    stage(unit)
        more = min(max(relay_done, RELAY[7] + int(PACE * (turn + 1))), bulk_done)
        relay_start(relay_done, more)
        relay_done = more
    assemble(1)

    arrived(pfar, pin, osem, orsem.at[0]).wait_send()
    arrived(amsg, ain, zsem, zrsem.at[0]).wait_send()
    arrived(fmsg, fin, fsem, frsem.at[0]).wait_send()
    arrived(ymsg, yin, ysem, yrsem.at[0]).wait_send()
    arrived(xin, sin, xsem, wrsem.at[0, 0]).wait_send()
    arrived(xin, sin, wsem, wrsem.at[0, 0]).wait_send()
    arrived(raw.at[0], raw.at[1], msem, mrsem.at[0]).wait_send()
    to_mate.wait_send()
    to_cousin.wait_send()


def whole(mesh, methyl, atlas, panel_ids):
    samps, probes_n = mesh.shape["samp"], mesh.shape["probe"]
    rows, cols = methyl.shape
    share, width = rows // probes_n, cols // samps
    phases = share // GROUP
    units = 3 * phases
    pieces = phases * (probes_n // PIECE)
    per_core = probes_n // 2
    vmem = pl.BlockSpec(memory_space=pltpu.VMEM)
    dma = pltpu.SemaphoreType.DMA
    return pl.pallas_call(
        functools.partial(program_kernel, samps, probes_n, rows * samps),
        out_shape=(
            jax.ShapeDtypeStruct((K, share), F32),
            jax.ShapeDtypeStruct((3, share, rows), F32),
        ),
        in_specs=[pl.BlockSpec(memory_space=pl.ANY), vmem, vmem],
        out_specs=(vmem,) * 2,
        scratch_shapes=[
            pltpu.VMEM((probes_n, share, cols), BF16),
            pltpu.VMEM((probes_n, 3 * K // 4, 128), F32),
            pltpu.VMEM((probes_n, 3 * K // 4, 128), F32),
            pltpu.VMEM((K, K, 128), F32),
            pltpu.VMEM((K // 2, 128), BF16),
            pltpu.VMEM((probes_n, K // 2, 128), BF16),
            pltpu.VMEM((samps, 5 * K // 4, width), F32),
            pltpu.VMEM((samps, 5 * K // 4, width), F32),
            pltpu.VMEM((K, width), F32),
            pltpu.VMEM((samps, K, width), F32),
            pltpu.VMEM((rows, cols), F32),
            pltpu.VMEM((1, cols), F32),
            pltpu.VMEM((samps, 1, cols), F32),
            pltpu.VMEM((4 * K, cols), BF16),
            pltpu.VMEM((K, rows), BF16),
            pltpu.VMEM((2, K, rows), BF16),
            pltpu.VMEM((2, probes_n, share, 4 * K), BF16),
            pltpu.VMEM((probes_n, share, cols), BF16),
            pltpu.VMEM((2, phases, probes_n, GROUP, cols // 2), BF16),
            pltpu.VMEM((units, per_core, GROUP, rows), F32),
            pltpu.VMEM((units, per_core, GROUP, rows), BF16),
            pltpu.VMEM((units, per_core, GROUP, rows), BF16),
            pltpu.VMEM((units, 2, 2, GROUP, rows), BF16),
            pltpu.VMEM((units, 2, 2, GROUP, rows), BF16),
            pltpu.VMEM((units, 2, GROUP, rows), BF16),
            pltpu.VMEM((units, 2, GROUP, rows), BF16),
            pltpu.VMEM((units, 2, GROUP, rows), F32),
            pltpu.VMEM((units, GROUP, rows), BF16),
            pltpu.VMEM((units, GROUP, rows), BF16),
            pltpu.VMEM((3, share, rows), F32),
            pltpu.VMEM((2, share, rows), BF16),
            pltpu.VMEM((2, phases // 2, per_core, 2 * GROUP, 2 * share), BF16),
            pltpu.VMEM((2, phases // 2, per_core, 2 * GROUP, 2 * share), BF16),
            pltpu.VMEM((probes_n, share, 4 * K), BF16),
            dma, dma, dma, dma, dma, dma, dma, dma, dma, dma,
            dma((2,)), dma((2,)), dma, dma((pieces,)), dma((pieces,)), dma((pieces,)),
            dma, dma((units,)), dma, dma((units,)), dma, dma((units,)), dma, dma((units,)),
            dma, dma((2, phases // 2)), dma, dma((2, phases // 2)), dma((4,)),
        ],
        compiler_params=pltpu.CompilerParams(
            collective_id=0, has_side_effects=True, vmem_limit_bytes=60 * 1024 * 1024
        ),
        name="whole",
    )(methyl.reshape(probes_n, share, cols), atlas, panel_ids.reshape(1, -1))


def solution(mesh):
    def body(methyl, atlas, panel_ids):
        scores, relmat = whole(mesh, methyl, atlas, panel_ids)
        return jnp.swapaxes(relmat, 1, 2), scores

    return jax.shard_map(
        body,
        mesh=mesh,
        in_specs=(P("samp", "probe"), P(None, "probe"), P()),
        out_specs=(P(None, "samp", "probe"), P(None, ("samp", "probe"))),
        check_vma=False,
    )
```
